128 devices in a mesh: seq: 32 (over x, z, core), head: 4 (over y).
Axes of the slice: x: 4, y: 4, z: 4, core: 2. Of those that a mesh axis runs over, the one named last changes fastest.
Arguments:
- inputs: bfloat16 [32768, 6144], P('seq'), may hold values from -6 to 6
- query_vectors: bfloat16 [32768, 4096], P('seq', 'head')
- key_vectors: bfloat16 [32768, 4096], P('seq', 'head'), may hold values from -6 to 6
- value_weight: bfloat16 [6144, 4096], P('seq', 'head'), may hold values from -0.078125 to 0.078125
- log_decay: float32 [32, 32768], P('head', 'seq'), may hold values from -0.8 to 0
- doc_start: int32 [128], P('seq'), may hold values 0 or 1
- norm_gain: float32 [4096], P('head'), may hold values from 0.1 to 1.9
Outputs:
- attended: bfloat16 [32768, 4096], P('seq', 'head')
The draws below stay inside these ranges and needn't reach their ends.
All inputs are finite; a program needn't handle non-finite values. No bound on the sum of `doc_start` on one device may be relied on, other than what follows from the above.
Results may differ from the reference program's by a relative error of at most 0.0053.
Values may be sent and summed in bfloat16 or wider, within the bound.
No kernel may reach another device: no remote copies, remote signals or barrier semaphores. Data moves between devices by JAX's collectives and lax.ppermute only.
A program may use at most 128 MiB of HBM per device.

```python
import math
import jax
import jax.numpy as jnp
from jax import lax

D = 6144
SHARD_ATTN_PARTS = 32
E = 128
SPAN = 256
TOK_DEV = 1024
SEQ_LENGTH_TOTAL = 32768
NCHUNK = 128


def draw_query_vectors(key, part):
    stochastic_child_seeds = jax.random.split(key, 2)
    column_head = jnp.arange(SHARD_ATTN_PARTS * E) // E
    jitter = jax.random.uniform(stochastic_child_seeds[0], (SHARD_ATTN_PARTS,), jnp.float32)
    head_scale = jnp.exp(math.log(10.0) * (column_head.astype(jnp.float32) + jitter[column_head]) / SHARD_ATTN_PARTS)
    base = jnp.clip(jax.random.normal(stochastic_child_seeds[1], (SEQ_LENGTH_TOTAL, SHARD_ATTN_PARTS * E), jnp.float32), -5.0, 5.0)
    return (base * head_scale[None, :]).astype(jnp.bfloat16)


def draw_log_decay(key, part):
    stochastic_child_seeds = jax.random.split(key, 7)
    fast_share = 0.5
    fast_heads = jax.random.uniform(stochastic_child_seeds[0], (SHARD_ATTN_PARTS, 1), jnp.float32) < fast_share
    fast_rates = 1.0 / jax.random.uniform(stochastic_child_seeds[1], (SHARD_ATTN_PARTS, 1), jnp.float32, 30.0, 50.0)
    slow_rates = jax.random.uniform(stochastic_child_seeds[2], (SHARD_ATTN_PARTS, 1), jnp.float32, 0.02, 0.3) / SEQ_LENGTH_TOTAL
    fading_speeds = jnp.where(fast_heads, fast_rates, slow_rates)
    shard_fading_multiplier = jax.random.uniform(stochastic_child_seeds[3], (SHARD_ATTN_PARTS, SEQ_LENGTH_TOTAL // TOK_DEV), jnp.float32, 0.5, 2.0)
    shard_fading_multiplier = jnp.repeat(shard_fading_multiplier, TOK_DEV, axis=1)
    approximate_guess = jax.random.uniform(stochastic_child_seeds[4], (SHARD_ATTN_PARTS, SEQ_LENGTH_TOTAL), jnp.float32, 0.5, 1.5)
    spike_clusters = jax.random.uniform(stochastic_child_seeds[5], (SHARD_ATTN_PARTS, SEQ_LENGTH_TOTAL), jnp.float32) < 2.0 / SEQ_LENGTH_TOTAL
    objective_numbers = jnp.log(jax.random.uniform(stochastic_child_seeds[6], (SHARD_ATTN_PARTS, SEQ_LENGTH_TOTAL), jnp.float32, 0.5, 0.8))
    ultimate_answer = -fading_speeds * shard_fading_multiplier * approximate_guess + jnp.where(spike_clusters, objective_numbers, 0.0)
    return ultimate_answer.astype(jnp.float32)


def set_ends(result, own_key, least, high):
    dims = result.shape
    place = [jax.random.randint(jax.random.fold_in(own_key, axis), (), 0, dims[axis]) for axis in range(len(dims))]
    result = result.at[tuple(place)].set(least)
    longest = dims.index(max(dims))
    place[longest] = (place[longest] + 1) % dims[longest]
    return result.at[tuple(place)].set(high)


def shard_levels(own_key, shape, shards, least, top_value):
    level = 1.0
    for axis_at, blocks in shards:
        steps = jax.random.uniform(jax.random.fold_in(jax.random.fold_in(own_key, 6), axis_at), (blocks,), jnp.float32, least / len(shards), top_value / len(shards))
        level = level * jnp.repeat(jnp.exp(steps), shape[axis_at] // blocks).reshape((-1,) + (1,) * (len(shape) - 1 - axis_at))
    return level


def noise(rng, shape, deviation, most, cuts=(), dtype=jnp.bfloat16):
    level = shard_levels(rng, shape, cuts, -0.22, 0.18) if cuts else 1.0
    values = jax.random.normal(rng, shape, jnp.float32) * deviation * level
    return jnp.minimum(jnp.maximum(values, -most), most).astype(dtype)


def setup_inputs(seed: int = 0) -> dict:
    key_list = jax.random.split(jax.random.key(seed), 8)
    return {
        "inputs": noise(key_list[0], (SEQ_LENGTH_TOTAL, D), 1.0, 6.0, ((0, 32),)),
        "query_vectors": draw_query_vectors(jax.random.fold_in(key_list[7], 71), 0),
        "key_vectors": noise(key_list[2], (SEQ_LENGTH_TOTAL, SHARD_ATTN_PARTS * E), 1.0, 6.0, ((0, 32), (1, 4))),
        "value_weight": noise(key_list[3], (D, SHARD_ATTN_PARTS * E), D ** -0.5, 0.078125, ((0, 32), (1, 4))),
        "log_decay": draw_log_decay(jax.random.fold_in(key_list[7], 71), 0),
        "doc_start": set_ends((jax.random.randint(key_list[5], (NCHUNK,), 0, 16) < 1).astype(jnp.int32), jax.random.fold_in(key_list[5], 1), 0, 1),
        "norm_gain": jnp.clip(1.0 + 0.18 * jax.random.normal(key_list[6], (SHARD_ATTN_PARTS * E,), jnp.float32), 0.1, 1.9),
    }


def reference(inputs, query_vectors, key_vectors, value_weight, log_decay, doc_start, norm_gain):
    values = jnp.dot(inputs, value_weight, preferred_element_type=jnp.float32).astype(jnp.bfloat16)
    query_blocks = query_vectors.reshape(NCHUNK, SPAN, SHARD_ATTN_PARTS, E)
    key_blocks = key_vectors.reshape(NCHUNK, SPAN, SHARD_ATTN_PARTS, E)
    value_blocks = values.reshape(NCHUNK, SPAN, SHARD_ATTN_PARTS, E)
    decay_blocks = jnp.transpose(log_decay.reshape(SHARD_ATTN_PARTS, NCHUNK, SPAN), (1, 0, 2))
    causal = lax.broadcasted_iota(jnp.int32, (SPAN, SPAN), 0) >= lax.broadcasted_iota(jnp.int32, (SPAN, SPAN), 1)

    def advance(memory, pieces):
        query_now, key_now, value_now, decay_now, starts = pieces
        memory = memory * (1 - starts).astype(jnp.float32)
        cumulative = jnp.cumsum(decay_now, axis=1)
        scores = jnp.einsum('ihe,jhe->hij', query_now.astype(jnp.float32), key_now.astype(jnp.float32))
        gaps = cumulative[:, :, None] - cumulative[:, None, :]
        weights = (scores * jnp.exp(jnp.where(causal[None], gaps, -1e+30))).astype(jnp.bfloat16)
        inner = jnp.einsum('hij,jhe->ihe', weights.astype(jnp.float32), value_now.astype(jnp.float32))
        query_decayed = query_now.astype(jnp.float32) * jnp.exp(cumulative).T[:, :, None]
        outer = jnp.einsum('ihe,hef->ihf', query_decayed, memory, precision=lax.Precision.HIGHEST)
        span_end = cumulative[:, -1]
        key_decayed = (key_now.astype(jnp.float32) * jnp.exp(span_end[:, None] - cumulative).T[:, :, None]).astype(jnp.bfloat16)
        update = jnp.einsum('jhe,jhf->hef', key_decayed.astype(jnp.float32), value_now.astype(jnp.float32), precision=lax.Precision.HIGHEST)
        memory = jnp.exp(span_end)[:, None, None] * memory + update
        return (memory, inner + outer)
    initial = jnp.zeros((SHARD_ATTN_PARTS, E, E), jnp.float32)
    final, outputs = lax.scan(advance, initial, (query_blocks, key_blocks, value_blocks, decay_blocks, doc_start))
    outputs = outputs.reshape(SEQ_LENGTH_TOTAL, SHARD_ATTN_PARTS * E)
    mean_square = lax.optimization_barrier(jnp.mean(outputs * outputs, axis=1, keepdims=True))
    return (outputs * lax.rsqrt(mean_square + 1e-06) * norm_gain[None, :]).astype(jnp.bfloat16)
```

```python
import functools
import jax
import jax.numpy as jnp
from jax import lax
from jax.experimental import pallas as pl
from jax.experimental.pallas import tpu as pltpu
from jax.sharding import Mesh, PartitionSpec as P

SHARD_ATTN_PARTS = 32
E = 128
SPAN = 256
SEQ = ("x", "z", "core")
SWAP = [(0, 1), (1, 0)]
VM = pl.BlockSpec(memory_space=pltpu.VMEM)
HB = pl.BlockSpec(memory_space=pltpu.HBM)
MIB = 1024 * 1024
HALF = 512
LINE = 1536
CHIP = 384
f32, bf16 = jnp.float32, jnp.bfloat16


def swap(a):
    return lax.ppermute(a, "core", SWAP)


def ring(a, axis, step):
    return lax.ppermute(a, axis, [(i, (i + step) % 4) for i in range(4)])


def crossed(a, first, second, step0, step1):
    pairs = []
    for x in range(4):
        for z in range(4):
            for c in range(2):
                axis, step = ((first, step0), (second, step1))[c]
                tx = (x + step) % 4 if axis == "x" else x
                tz = (z + step) % 4 if axis == "z" else z
                pairs.append((x * 8 + z * 2 + c, tx * 8 + tz * 2 + c))
    return lax.ppermute(a, SEQ, pairs)


def dot(a, b, dims=((1,), (0,))):
    return lax.dot_general(a, b, (dims, ((), ())), preferred_element_type=f32)


def split_dot(a, m):
    high = m.astype(bf16)
    low = (m - high.astype(f32)).astype(bf16)
    return dot(a, high) + dot(a, low)


def block_cum(ld):
    lane = lax.broadcasted_iota(jnp.int32, ld.shape, 1)
    step = 1
    while step < SPAN:
        ld = ld + jnp.where(lane >= step, pltpu.roll(ld, step, 1), 0.0)
        step *= 2
    return ld


def vmem(a):
    return pltpu.with_memory_space_constraint(a, pltpu.VMEM)


def hbm(a):
    return pltpu.with_memory_space_constraint(a, pltpu.HBM)


def params(mib):
    return pltpu.CompilerParams(vmem_limit_bytes=mib * MIB)


def pre_kernel(ld_ref, q_hbm, k_hbm, w_hbm, kd_hbm, q_ref, k_ref, w_ref, kd_ref, sems):
    half = SPAN // 2
    low = lax.broadcasted_iota(jnp.int32, (half, half), 0) >= lax.broadcasted_iota(
        jnp.int32, (half, half), 1
    )

    def loads(h):
        lanes = pl.ds(pl.multiple_of(h * E, E), E)
        return (
            pltpu.make_async_copy(q_hbm.at[:, lanes], q_ref.at[:, lanes], sems.at[0, h]),
            pltpu.make_async_copy(k_hbm.at[:, lanes], k_ref.at[:, lanes], sems.at[1, h]),
        )

    def stores(h):
        lanes = pl.ds(pl.multiple_of(h * E, E), E)
        return (
            pltpu.make_async_copy(w_ref.at[h], w_hbm.at[h], sems.at[2, h]),
            pltpu.make_async_copy(kd_ref.at[:, lanes], kd_hbm.at[:, lanes], sems.at[3, h]),
        )

    for h in range(8):
        for c in loads(h):
            c.start()
    w_ref[:, :, :half, half:] = jnp.zeros((8, 4, half, half), bf16)
    cums = [block_cum(ld_ref[:, b * SPAN : (b + 1) * SPAN]) for b in range(4)]

    def one_head(h, carry):
        for c in loads(h):
            c.wait()
        head = lax.broadcasted_iota(jnp.int32, (8, SPAN), 0) == h
        lanes = pl.ds(pl.multiple_of(h * E, E), E)
        for b in range(4):
            row = jnp.sum(jnp.where(head, cums[b], 0.0), axis=0, keepdims=True)
            col = jnp.transpose(jnp.broadcast_to(row, (8, SPAN)))[:, 0:1]
            last = row[:, SPAN - 1 : SPAN]
            rows = slice(b * SPAN, (b + 1) * SPAN)
            k = k_ref[rows, lanes]
            kd_ref[rows, lanes] = (k.astype(f32) * jnp.exp(last - col)).astype(bf16)
            q = q_ref[rows, lanes]
            s = dot(q[:half], k[:half], ((1,), (1,)))
            g = jnp.exp(jnp.where(low, col[:half] - row[:, :half], -1e30))
            w_ref[h, b, :half, :half] = (s * g).astype(bf16)
            s = dot(q[half:], k, ((1,), (1,)))
            g = jnp.exp(col[half:] - row[:, :half])
            w_ref[h, b, half:, :half] = (s[:, :half] * g).astype(bf16)
            g = jnp.exp(jnp.where(low, col[half:] - row[:, half:], -1e30))
            w_ref[h, b, half:, half:] = (s[:, half:] * g).astype(bf16)
        for c in stores(h):
            c.start()
        return carry

    lax.fori_loop(0, 8, one_head, 0)
    for h in range(8):
        for c in stores(h):
            c.wait()


def pre(ld, q, k):
    shapes = ((8, 4, SPAN, SPAN), (1024, 1024))
    return pl.pallas_call(
        pre_kernel,
        in_specs=[VM, HB, HB],
        out_specs=[HB] * 2,
        out_shape=[pltpu.HBM(s, bf16) for s in shapes],
        scratch_shapes=[pltpu.VMEM((1024, 1024), bf16)] * 2
        + [pltpu.VMEM(s, bf16) for s in shapes]
        + [pltpu.SemaphoreType.DMA((4, 8))],
        compiler_params=params(20),
        cost_estimate=pl.CostEstimate(flops=10**9, transcendentals=2 * 10**6, bytes_accessed=10**7),
        name="pre",
    )(ld, hbm(q), hbm(k))


def input_copies(jobs, x_hbm, xv, sems):
    x, z, core = lax.axis_index("x"), lax.axis_index("z"), lax.axis_index("core")
    out = []
    for j, (mine, d) in enumerate(jobs):
        first = (core == 0) if mine else (core == 1)
        line = lax.rem(jnp.where(first, x, z) + 4 - d, 4)
        cs = []
        for e in range(4):
            other = lax.rem(jnp.where(first, z, x) + 4 - e, 4)
            at = jnp.where(first, line * LINE + other * CHIP, other * LINE + line * CHIP)
            cs.append(
                pltpu.make_async_copy(
                    x_hbm.at[:, pl.ds(pl.multiple_of(at, 128), CHIP)],
                    xv.at[j, :, pl.ds(e * CHIP, CHIP)],
                    sems.at[j, e],
                )
            )
        out.append(cs)
    return out


def multiply(j, xv, lo, hi, src, dst):
    for r in range(2):
        rows = slice(r * 512, (r + 1) * 512)
        part = dot(xv[j, rows, : 2 * CHIP], lo[...]) + dot(xv[j, rows, 2 * CHIP :], hi[...])
        if src is not None:
            part = part + src[rows, :]
        dst[rows, :] = part


def mm_kernel(jobs, ahead, has_acc, keep, x_hbm, *refs):
    n = 2 * len(jobs)
    refs = list(refs)
    take = lambda k: [refs.pop(0) for _ in range(k)]
    sides = [mine for mine, _ in jobs]
    halves = list(dict.fromkeys(sides))
    bufs = take(n)
    srcs = take(1) if has_acc else []
    outs = dict(zip(halves, take(len(halves))))
    nxt = take(1)[0] if ahead else None
    xv, sems, wv, wsems = take(4)
    acc, asems = take(2)
    lsems = take(1)[0] if ahead else None
    copies = input_copies(jobs, x_hbm, xv, sems)
    for i in range(n):
        copies[i // 2].append(pltpu.make_async_copy(bufs[i], wv.at[i], wsems.at[i]))
    for cs in copies:
        for c in cs:
            c.start()
    held = [pltpu.make_async_copy(s, acc.at[i], asems.at[i]) for i, s in enumerate(srcs)]
    for c in held:
        c.start()
    later = input_copies(ahead, x_hbm, nxt, lsems) if ahead else []
    for cs in later:
        for c in cs:
            c.start()
    for c in held:
        c.wait()
    seen = set()
    back = []
    for j, mine in enumerate(sides):
        for c in copies[j]:
            c.wait()
        i = halves.index(mine)
        dst = outs[mine] if keep else acc.at[i]
        src = dst if mine in seen else (acc.at[i] if has_acc else None)
        multiply(j, xv, wv.at[2 * j], wv.at[2 * j + 1], src, dst)
        seen.add(mine)
        if not keep and mine not in sides[j + 1 :]:
            back.append(pltpu.make_async_copy(acc.at[i], outs[mine], asems.at[i]))
            back[-1].start()
    for c in back:
        c.wait()
    for cs in later:
        for c in cs:
            c.wait()


def mm(jobs, ahead, keep, x, bufs, acc=None):
    n = len(jobs)
    halves = len(dict.fromkeys(mine for mine, _ in jobs))
    outs = [(pltpu.VMEM if keep else pltpu.HBM)((1024, HALF), f32)] * halves
    ospecs = [VM if keep else HB] * halves
    scratch = [
        pltpu.VMEM((n, 1024, LINE), bf16),
        pltpu.SemaphoreType.DMA((n, 4)),
        pltpu.VMEM((2 * n, 2 * CHIP, HALF), bf16),
        pltpu.SemaphoreType.DMA((2 * n,)),
        pltpu.VMEM((halves, 1024, HALF), f32),
        pltpu.SemaphoreType.DMA((halves,)),
    ]
    if ahead:
        outs.append(pltpu.VMEM((len(ahead), 1024, LINE), bf16))
        ospecs.append(VM)
        scratch.append(pltpu.SemaphoreType.DMA((len(ahead), 4)))
    extra = [] if acc is None else [hbm(acc)]
    return pl.pallas_call(
        functools.partial(mm_kernel, jobs, ahead, acc is not None, keep),
        in_specs=[HB] * (1 + len(bufs) + len(extra)),
        out_specs=ospecs,
        out_shape=outs,
        scratch_shapes=scratch,
        compiler_params=params(6 + 6 * n),
        cost_estimate=pl.CostEstimate(
            flops=2 * 1024 * LINE * HALF * n,
            transcendentals=0,
            bytes_accessed=n * 5 * 10**6,
        ),
        name="project",
    )(hbm(x), *[hbm(a) for a in bufs], *extra)


def head_col(ld_block):
    return jnp.transpose(jnp.exp(block_cum(ld_block)))


def post_kernel(jobs, dec, ld_ref, q_hbm, kd_hbm, w_hbm, mine_ref, their_ref, xv, *refs):
    bufs = refs[: 2 * len(jobs)]
    comb_hbm, keep_ref, give_ref, acc, q_ref, kd_ref, w_ref, comb_ref, sems, osems = refs[
        2 * len(jobs) :
    ]
    core = lax.axis_index("core")
    loads = [
        pltpu.make_async_copy(s, t, sems.at[i])
        for i, (s, t) in enumerate(((q_hbm, q_ref), (kd_hbm, kd_ref), (w_hbm, w_ref)))
    ]
    for c in loads:
        c.start()
    cols = [head_col(ld_ref[:, b * SPAN : (b + 1) * SPAN]) for b in range(4)]
    for j, (mine, _) in enumerate(jobs):
        src, half = (mine_ref, core) if mine else (their_ref, 1 - core)
        multiply(j, xv, bufs[2 * j], bufs[2 * j + 1], src, acc.at[half])
    for c in loads:
        c.wait()
    half = SPAN // 2
    stores = []
    for h in range(8):
        lanes = slice(h * E, (h + 1) * E)
        part = slice((h % 4) * E, (h % 4 + 1) * E)
        state = None
        for b in range(4):
            rows = slice(b * SPAN, (b + 1) * SPAN)
            v = acc[h // 4, rows, part].astype(bf16)
            top = dot(w_ref[h, b, :half, :half], v[:half])
            low = dot(w_ref[h, b, half:, :], v)
            inner = jnp.concatenate([top, low], axis=0)
            if b > 0:
                state = state * dec[32 + b : 33 + b, :]
                inner = inner + cols[b][:, h : h + 1] * split_dot(q_ref[rows, lanes], state)
            comb_ref[rows, lanes] = inner
            update = dot(kd_ref[rows, lanes], v, ((0,), (0,)))
            state = update if b == 0 else dec[h * 4 + b : h * 4 + b + 1, :] * state + update

        @pl.when(core == h // 4)
        def _():
            keep_ref[part, :] = state

        @pl.when(core != h // 4)
        def _():
            give_ref[part, :] = state

        stores.append(
            pltpu.make_async_copy(comb_ref.at[:, lanes], comb_hbm.at[:, lanes], osems.at[h])
        )
        stores[-1].start()
    for c in stores:
        c.wait()


def post(jobs, dec, ld, q, kd, w, mine, theirs, xv, bufs):
    return pl.pallas_call(
        functools.partial(post_kernel, jobs),
        in_specs=[VM, VM, HB, HB, HB] + [VM] * (3 + len(bufs)),
        out_specs=[HB, VM, VM],
        out_shape=[
            pltpu.HBM((1024, 1024), f32),
            pltpu.VMEM((HALF, E), f32),
            pltpu.VMEM((HALF, E), f32),
        ],
        scratch_shapes=[
            pltpu.VMEM((2, 1024, HALF), f32),
            pltpu.VMEM((1024, 1024), bf16),
            pltpu.VMEM((1024, 1024), bf16),
            pltpu.VMEM((8, 4, SPAN, SPAN), bf16),
            pltpu.VMEM((1024, 1024), f32),
            pltpu.SemaphoreType.DMA((3,)),
            pltpu.SemaphoreType.DMA((8,)),
        ],
        compiler_params=params(24),
        name="post",
    )(dec, ld, hbm(q), hbm(kd), hbm(w), mine, theirs, xv, *bufs)


def chip_kernel(cw, own_ref, recv_ref, f_ref, b_ref):
    for h in range(4):
        r = slice(h * E, (h + 1) * E)
        s = cw[h : h + 1, :] * own_ref[r, :] + cw[4 + h : 5 + h, :] * recv_ref[r, :]
        f_ref[r, :] = s
        b_ref[r, :] = s.astype(bf16)


def spread_kernel(sw, own_ref, r1, r2, r3, o0, o1, o2, o3):
    for h in range(4):
        r = slice(h * E, (h + 1) * E)
        src = [own_ref[r, :]] + [a[r, :].astype(f32) for a in (r1, r2, r3)]
        for d, o in enumerate((o0, o1, o2, o3)):
            s = None
            for e in range(4):
                at = (d * 4 + e) * 4 + h
                t = sw[at : at + 1, :] * src[e]
                s = t if s is None else s + t
            o[r, :] = s.astype(o.dtype)


def enter_kernel(ew, m0, r1, r2, r3, own_ref, recv_ref, mine_ref, other_ref):
    for h in range(4):
        r = slice(h * E, (h + 1) * E)
        i = m0[r, :]
        for a in (r1, r2, r3):
            i = i + a[r, :].astype(f32)
        w = [ew[4 * n + h : 4 * n + h + 1, :] for n in range(4)]
        mine_ref[r, :] = w[0] * i + w[1] * recv_ref[r, :]
        other_ref[r, :] = w[2] * i + w[3] * own_ref[r, :]


def small(kernel, name, args, outs):
    return pl.pallas_call(
        kernel,
        in_specs=[VM] * len(args),
        out_specs=[VM] * len(outs),
        out_shape=[pltpu.VMEM((HALF, E), t) for t in outs],
        compiler_params=params(4),
        name=name,
    )(*args)


def outer_kernel(
    sf, ld_ref, mine_ref, other_ref, q_hbm, comb_hbm, out_ref, sq_ref, q_ref, comb_ref, sems
):
    loads = []
    for b in range(4):
        rows = slice(b * SPAN, (b + 1) * SPAN)
        loads.append(
            [
                pltpu.make_async_copy(q_hbm.at[rows, :], q_ref.at[rows, :], sems.at[0, b]),
                pltpu.make_async_copy(comb_hbm.at[rows, :], comb_ref.at[rows, :], sems.at[1, b]),
            ]
        )
        for c in loads[b]:
            c.start()
    first = lax.axis_index("core") == 0
    high, low = [], []
    for h in range(8):
        r = slice((h % 4) * E, (h % 4 + 1) * E)
        a, b = mine_ref[r, :], other_ref[r, :]
        m = jnp.where(first, a, b) if h < 4 else jnp.where(first, b, a)
        high.append(m.astype(bf16))
        low.append((m - high[h].astype(f32)).astype(bf16))
    for b in range(4):
        for c in loads[b]:
            c.wait()
        rows = slice(b * SPAN, (b + 1) * SPAN)
        col = head_col(ld_ref[:, rows]) * sf[b : b + 1, :]
        total = None
        for h in range(8):
            lanes = slice(h * E, (h + 1) * E)
            q = q_ref[rows, lanes]
            o = (dot(q, high[h]) + dot(q, low[h])) * col[:, h : h + 1]
            o = comb_ref[rows, lanes] + o
            out_ref[rows, lanes] = o
            total = o * o if total is None else total + o * o
        for t in range(2):
            tt = jnp.transpose(total[t * E : (t + 1) * E, :])
            sq_ref[b * 2 + t : b * 2 + t + 1, :] = jnp.sum(tt, axis=0, keepdims=True)


def outer(sf, ld, q, mine, other, comb):
    return pl.pallas_call(
        outer_kernel,
        in_specs=[VM] * 4 + [HB] * 2,
        out_specs=[VM, VM],
        out_shape=[pltpu.VMEM((1024, 1024), f32), pltpu.VMEM((8, E), f32)],
        scratch_shapes=[
            pltpu.VMEM((1024, 1024), bf16),
            pltpu.VMEM((1024, 1024), f32),
            pltpu.SemaphoreType.DMA((2, 4)),
        ],
        compiler_params=params(12),
        name="outer",
    )(sf, ld, mine, other, hbm(q), hbm(comb))


def norm_kernel(out_ref, s0, s1, s2, s3, gain_ref, y_hbm, y_ref, sems):
    total = s0[...] + s1[...] + s2[...] + s3[...]
    scale = lax.rsqrt(total / (SHARD_ATTN_PARTS * E) + 1e-06)
    copies = []
    for t in range(8):
        col = jnp.transpose(jnp.broadcast_to(scale[t : t + 1, :], (E, E)))
        rows = slice(t * E, (t + 1) * E)
        for h in range(8):
            lanes = slice(h * E, (h + 1) * E)
            y_ref[rows, lanes] = (out_ref[rows, lanes] * col * gain_ref[:, lanes]).astype(bf16)
        c = pltpu.make_async_copy(y_ref.at[rows, :], y_hbm.at[rows, :], sems.at[t])
        c.start()
        copies.append(c)
    for c in copies:
        c.wait()


def norm(out, sqs, gain):
    return pl.pallas_call(
        norm_kernel,
        in_specs=[VM] * 6,
        out_specs=HB,
        out_shape=jax.ShapeDtypeStruct((1024, 1024), bf16),
        scratch_shapes=[pltpu.VMEM((1024, 1024), bf16), pltpu.SemaphoreType.DMA((8,))],
        compiler_params=params(8),
        name="norm",
    )(out, *sqs, gain)


def rows_of(a):
    return jnp.broadcast_to(a.reshape(-1, 1), (a.size, E))


def per_device(inputs, q, k, value_weight, ld, doc_start, gain):
    x, z, core = lax.axis_index("x"), lax.axis_index("z"), lax.axis_index("core")
    first = core == 0
    bar = lax.optimization_barrier

    my_w = lax.dynamic_slice(value_weight, (0, core * HALF), (CHIP // 2, HALF))
    their_w = lax.dynamic_slice(value_weight, (0, (1 - core) * HALF), (CHIP // 2, HALF))
    recv_w = swap(their_w)
    chip_w = jnp.where(
        first,
        jnp.concatenate([my_w, recv_w], axis=0),
        jnp.concatenate([recv_w, my_w], axis=0),
    )
    chip_w, ld, q, k = bar((chip_w, ld, q, k))
    line = [chip_w] + [crossed(chip_w, "z", "x", d, d) for d in (1, 2, 3)]

    sums = jnp.sum(ld.reshape(8, 4, SPAN), axis=2)
    bd = jnp.exp(sums)
    surv = 1.0 - doc_start.astype(f32)
    fac = bd * surv[None, :]
    f_own = jnp.prod(fac, axis=1)
    f_oth = swap(f_own)
    g = (f_own * f_oth)[None]

    def pair(g, axis, bit):
        return jnp.concatenate(
            [g, lax.ppermute(g, axis, [(i, i ^ bit) for i in range(4)])], axis=0
        )

    w, kd = pre(ld, q, k)
    g = pair(g, "z", 1)

    line, w, g = bar((tuple(line), w, g))
    p_lo = jnp.concatenate(line[:2], axis=0)
    p_hi = jnp.concatenate(line[2:], axis=0)
    up_lo = crossed(p_lo, "x", "z", 1, 1)
    dn_hi = crossed(p_hi, "x", "z", -1, -1)
    up_hi = crossed(p_hi, "x", "z", 1, 1)
    dn_lo = crossed(p_lo, "x", "z", -1, -1)
    mine, theirs = mm(
        ((True, 0), (False, 0)), (), False, inputs, (p_lo, p_hi, swap(p_lo), swap(p_hi))
    )
    up_lo, dn_hi, mine, theirs, g = bar((up_lo, dn_hi, mine, theirs, g))
    op_lo = crossed(up_lo, "x", "z", 1, 1)
    op_hi = crossed(dn_hi, "x", "z", -1, -1)
    g = pair(g, "z", 2)

    def my_heads(a):
        return jnp.where(first, a[..., :4], a[..., 4:])

    fo, ft = my_heads(f_own), my_heads(f_oth)
    one, zero = jnp.ones((4,), f32), jnp.zeros((4,), f32)
    cw = rows_of(jnp.where(first, jnp.concatenate([ft, one]), jnp.concatenate([one, fo])))
    ew = rows_of(
        jnp.where(
            first,
            jnp.concatenate([one, zero, fo, one]),
            jnp.concatenate([ft, one, one, zero]),
        )
    )
    dec = jnp.concatenate([rows_of(bd), rows_of(surv), jnp.zeros((4, E), f32)], axis=0)
    sf = jnp.stack([surv[b] * jnp.prod(fac[:, :b], axis=1) for b in range(4)], axis=0)

    bufs = [up_lo, up_hi, dn_lo, dn_hi]
    mine = mm(((True, 1), (True, 3)), (), True, inputs, bufs, mine)[0]
    mine, g, bufs = bar((mine, g, tuple(swap(a) for a in bufs)))
    g = pair(g, "x", 1)
    last = ((True, 2), (False, 2))
    theirs, xv = mm(((False, 1), (False, 3)), last, True, inputs, bufs, theirs)
    theirs, cw, ew, dec, sf, g = bar((theirs, cw, ew, dec, sf, g))
    g16 = pair(g, "x", 2)
    bufs = [op_lo, op_hi, swap(op_lo), swap(op_hi)]
    comb, own, give = post(
        last, vmem(dec), ld, q, kd, w, mine, theirs, xv, [vmem(a) for a in bufs]
    )
    give, g16 = bar((give, g16))
    off = jnp.arange(4)
    k_at = ((x ^ off)[:, None] * 4 + (z ^ off)[None, :]).reshape(16)
    src = jnp.where(first, x * 4 + (z - off) % 4, ((x - off) % 4) * 4 + z)
    tgt = jnp.where(first, ((x + off) % 4) * 4 + z, x * 4 + (z + off) % 4)
    between = (k_at[None, None, :] > src[None, :, None]) & (
        k_at[None, None, :] < tgt[:, None, None]
    )
    w16 = jnp.prod(jnp.where(between[..., None], my_heads(g16)[None, None], 1.0), axis=2)
    w16 = jnp.where((src[None, :] < tgt[:, None])[..., None], w16, 0.0)
    sw = rows_of(w16)

    recv = vmem(swap(give))
    chip, chip16 = small(chip_kernel, "chip", (vmem(cw), own, recv), (f32, bf16))
    got = [vmem(crossed(chip16, "z", "x", d, d)) for d in (1, 2, 3)]
    sent = small(spread_kernel, "spread", (vmem(sw), chip, *got), (f32, bf16, bf16, bf16))
    got = [vmem(crossed(sent[d], "x", "z", d, d)) for d in (1, 2, 3)]
    mine, give = small(
        enter_kernel, "enter", (vmem(ew), sent[0], *got, own, recv), (f32, f32)
    )
    other = vmem(swap(give))
    out, sq = outer(vmem(sf), ld, q, mine, other, comb)
    sqs = [sq] + [vmem(ring(sq, "head", d)) for d in (1, 2, 3)]
    return norm(out, sqs, gain.reshape(1, -1))


def solution(mesh):
    mesh = Mesh(mesh.devices.reshape(4, 4, 2, 4), ("x", "z", "core", "head"))
    placed = (
        P(SEQ, None),
        P(SEQ, "head"),
        P(SEQ, "head"),
        P(SEQ, "head"),
        P("head", SEQ),
        P(SEQ),
        P("head"),
    )
    return jax.shard_map(
        per_device, mesh=mesh, in_specs=placed, out_specs=P(SEQ, "head"), check_vma=False
    )
```

```python
import functools
import jax
import jax.numpy as jnp
from jax import lax
from jax.experimental import pallas as pl
from jax.experimental.pallas import tpu as pltpu
from jax.sharding import Mesh, PartitionSpec as P

SHARD_ATTN_PARTS = 32
E = 128
SPAN = 256
SEQ = ("x", "z", "core")
SWAP = [(0, 1), (1, 0)]
VM = pl.BlockSpec(memory_space=pltpu.VMEM)
HB = pl.BlockSpec(memory_space=pltpu.HBM)
MIB = 1024 * 1024
HALF = 512
LINE = 1536
CHIP = 384
ROOM = 2
ROOM_P = 4
f32, bf16 = jnp.float32, jnp.bfloat16


def swap(a):
    return lax.ppermute(a, "core", SWAP)


def ring(a, axis, step):
    return lax.ppermute(a, axis, [(i, (i + step) % 4) for i in range(4)])


def crossed(a, first, second, step0, step1):
    pairs = []
    for x in range(4):
        for z in range(4):
            for c in range(2):
                axis, step = ((first, step0), (second, step1))[c]
                tx = (x + step) % 4 if axis == "x" else x
                tz = (z + step) % 4 if axis == "z" else z
                pairs.append((x * 8 + z * 2 + c, tx * 8 + tz * 2 + c))
    return lax.ppermute(a, SEQ, pairs)


def dot(a, b, dims=((1,), (0,))):
    return lax.dot_general(a, b, (dims, ((), ())), preferred_element_type=f32)


def block_cum(ld):
    lane = lax.broadcasted_iota(jnp.int32, ld.shape, 1)
    step = 1
    while step < SPAN:
        ld = ld + jnp.where(lane >= step, pltpu.roll(ld, step, 1), 0.0)
        step *= 2
    return ld


def vmem(a):
    return pltpu.with_memory_space_constraint(a, pltpu.VMEM)


def hbm(a):
    return pltpu.with_memory_space_constraint(a, pltpu.HBM)


def params(mib):
    return pltpu.CompilerParams(vmem_limit_bytes=mib * MIB)


def prep_kernel(doc, ld_ref, fx_ref, dec_ref, sf_ref):
    lane = lax.broadcasted_iota(jnp.int32, (E, E), 1)
    mat = jnp.zeros((E, E), f32)
    surv = []
    for b in range(4):
        total = jnp.sum(ld_ref[:, b * SPAN : (b + 1) * SPAN], axis=1, keepdims=True)
        decay = jnp.broadcast_to(jnp.exp(total), (8, E))
        dec_ref[b * 8 : b * 8 + 8, :] = decay
        tall = jnp.concatenate([decay, jnp.zeros((E - 8, E), f32)], axis=0)
        mat = jnp.where(lane == b, tall, mat)
        surv.append(1.0 - jnp.full((1, E), doc[b], jnp.int32).astype(f32))
    dec_ref[32:40, :] = jnp.concatenate(surv + [jnp.zeros((4, E), f32)], axis=0)
    rows = jnp.transpose(mat)
    f = None
    sfs = []
    for b in range(4):
        f = surv[b] if b == 0 else f * surv[b]
        sfs.append(f)
        f = f * rows[b : b + 1, :]
    sf_ref[...] = jnp.concatenate(sfs + [jnp.zeros((4, E), f32)], axis=0)
    high = f.astype(bf16).astype(f32)
    mid = (f - high).astype(bf16).astype(f32)
    low = f - high - mid
    tile = jnp.concatenate([high, mid, low, jnp.zeros((13, E), f32)], axis=0)
    fx_ref[:, E:] = jnp.zeros((16, HALF - E), bf16)
    fx_ref[:, :E] = tile.astype(bf16)


def prep(doc, ld):
    return pl.pallas_call(
        prep_kernel,
        in_specs=[pl.BlockSpec(memory_space=pltpu.SMEM), VM],
        out_specs=[VM] * 3,
        out_shape=[
            pltpu.VMEM((16, HALF), bf16),
            jax.ShapeDtypeStruct((40, E), f32),
            jax.ShapeDtypeStruct((8, E), f32),
        ],
        compiler_params=params(4),
        name="prep",
    )(doc, ld)


def pre_kernel(
    ld_ref, q_hbm, k_hbm, x_hbm, w_hbm, kd_hbm, x_ref, q_ref, k_ref, w_ref, kd_ref, sems, xsems
):
    half = SPAN // 2
    low = lax.broadcasted_iota(jnp.int32, (half, half), 0) >= lax.broadcasted_iota(
        jnp.int32, (half, half), 1
    )

    def loads(h):
        lanes = pl.ds(pl.multiple_of(h * E, E), E)
        return (
            pltpu.make_async_copy(q_hbm.at[:, lanes], q_ref.at[:, lanes], sems.at[0, h]),
            pltpu.make_async_copy(k_hbm.at[:, lanes], k_ref.at[:, lanes], sems.at[1, h]),
        )

    def stores(h):
        return (
            pltpu.make_async_copy(w_ref.at[h], w_hbm.at[h], sems.at[2, h]),
            pltpu.make_async_copy(kd_ref.at[h], kd_hbm.at[h], sems.at[3, h]),
        )

    for h in range(8):
        for c in loads(h):
            c.start()
    inputs = []
    for r in range(8):
        rows = slice(r * E, (r + 1) * E)
        inputs.append(
            pltpu.make_async_copy(x_hbm.at[rows, :], x_ref.at[rows, :], xsems.at[r])
        )
        inputs[r].start()
    w_ref[:, :, :half, half:] = jnp.zeros((8, 4, half, half), bf16)
    cums = [block_cum(ld_ref[:, b * SPAN : (b + 1) * SPAN]) for b in range(4)]

    def one_head(h, carry):
        for c in loads(h):
            c.wait()
        head = lax.broadcasted_iota(jnp.int32, (8, SPAN), 0) == h
        lanes = pl.ds(pl.multiple_of(h * E, E), E)
        for b in range(4):
            row = jnp.sum(jnp.where(head, cums[b], 0.0), axis=0, keepdims=True)
            col = jnp.transpose(jnp.broadcast_to(row, (8, SPAN)))[:, 0:1]
            last = row[:, SPAN - 1 : SPAN]
            rows = slice(b * SPAN, (b + 1) * SPAN)
            k = k_ref[rows, lanes]
            kt = jnp.transpose(k.astype(f32))
            kd_ref[h, b] = (kt * jnp.exp(last - row)).astype(bf16)
            q = q_ref[rows, lanes]
            s = dot(q[:half], k[:half], ((1,), (1,)))
            g = jnp.exp(jnp.where(low, col[:half] - row[:, :half], -1e30))
            w_ref[h, b, :half, :half] = (s * g).astype(bf16)
            s = dot(q[half:], k, ((1,), (1,)))
            g = jnp.exp(col[half:] - row[:, :half])
            w_ref[h, b, half:, :half] = (s[:, :half] * g).astype(bf16)
            g = jnp.exp(jnp.where(low, col[half:] - row[:, half:], -1e30))
            w_ref[h, b, half:, half:] = (s[:, half:] * g).astype(bf16)
        for c in stores(h):
            c.start()
        return carry

    lax.fori_loop(0, 8, one_head, 0)
    for h in range(8):
        for c in stores(h):
            c.wait()
    for c in inputs:
        c.wait()


def pre(ld, q, k, x):
    shapes = ((8, 4, SPAN, SPAN), (8, 4, E, SPAN))
    return pl.pallas_call(
        pre_kernel,
        in_specs=[VM, HB, HB, HB],
        out_specs=[HB, HB, VM],
        out_shape=[pltpu.HBM(s, bf16) for s in shapes] + [pltpu.VMEM(x.shape, bf16)],
        scratch_shapes=[pltpu.VMEM((1024, 1024), bf16)] * 2
        + [pltpu.VMEM(s, bf16) for s in shapes]
        + [pltpu.SemaphoreType.DMA((4, 8)), pltpu.SemaphoreType.DMA((8,))],
        compiler_params=params(14),
        cost_estimate=pl.CostEstimate(flops=10**9, transcendentals=2 * 10**6, bytes_accessed=10**7),
        name="pre",
    )(ld, hbm(q), hbm(k), hbm(x))


def multiply(mine, d, x_ref, lo, hi, src, dst):
    x, z, core = lax.axis_index("x"), lax.axis_index("z"), lax.axis_index("core")
    first = (core == 0) if mine else (core == 1)
    line = lax.rem(jnp.where(first, x, z) + 4 - d, 4)
    spans = []
    for e in range(4):
        other = lax.rem(jnp.where(first, z, x) + 4 - e, 4)
        at = jnp.where(first, line * LINE + other * CHIP, other * LINE + line * CHIP)
        spans.append(pl.ds(pl.multiple_of(at, 128), CHIP))
    for r in range(2):
        rows = slice(r * 512, (r + 1) * 512)
        part = src[rows, :] if src is not None else None
        for w, (s0, s1) in ((lo, spans[:2]), (hi, spans[2:])):
            lhs = jnp.concatenate([x_ref[rows, s0], x_ref[rows, s1]], axis=1)
            p = dot(lhs, w[: 2 * CHIP, :])
            part = p if part is None else part + p
        dst[rows, :] = part


def mm_kernel(jobs, tails, plane, x_ref, *refs):
    n = 2 * len(jobs)
    bufs, refs = refs[:n], refs[n:]
    src = refs[0].at[plane] if plane is not None else None
    out = refs[0 if plane is None else 1]
    wv, sems = refs[-2:]
    copies = [
        pltpu.make_async_copy(b.at[: 2 * CHIP, :], wv.at[i], sems.at[i])
        for i, b in enumerate(bufs)
    ]
    if tails:
        for j in range(len(jobs)):
            copies.append(
                pltpu.make_async_copy(
                    bufs[2 * j].at[2 * CHIP :, :E], refs[-3].at[j], sems.at[n + j]
                )
            )
    for c in copies:
        c.start()
    for j, (mine, d) in enumerate(jobs):
        copies[2 * j].wait()
        copies[2 * j + 1].wait()
        if plane is None:
            dst, before = out.at[j], None
        else:
            dst, before = out, (out if j else src)
        multiply(mine, d, x_ref, wv.at[2 * j], wv.at[2 * j + 1], before, dst)
    for c in copies[n:]:
        c.wait()


def mm(jobs, x, bufs, tails, plane=None, before=None):
    n = 2 * len(jobs)
    outs = [pltpu.VMEM((ROOM_P, 1024, HALF) if plane is None else (1024, HALF), f32)]
    if tails:
        outs.append(pltpu.VMEM((len(jobs), 64, E), bf16))
    extra = [] if before is None else [before]
    return pl.pallas_call(
        functools.partial(mm_kernel, jobs, tails, plane),
        in_specs=[VM] + [HB] * n + [VM] * len(extra),
        out_specs=[VM] * len(outs),
        out_shape=outs,
        scratch_shapes=[
            pltpu.VMEM((n, 2 * CHIP, HALF), bf16),
            pltpu.SemaphoreType.DMA((n + len(jobs),)),
        ],
        compiler_params=params(10),
        cost_estimate=pl.CostEstimate(
            flops=1024 * LINE * HALF * n, transcendentals=0, bytes_accessed=n * 5 * 10**6
        ),
        name="project",
    )(x, *[hbm(a) for a in bufs], *extra)


def head_col(ld_block):
    return jnp.transpose(jnp.exp(block_cum(ld_block)))


def post_kernel(jobs, dec, q_hbm, kd_hbm, w_hbm, mine_ref, their_ref, x_ref, *refs):
    bufs = refs[: 2 * len(jobs)]
    v_ref, keep_ref, give_ref, tail_ref, st_ref, q_ref, w_ref, acc, kd_ref, sems = refs[
        2 * len(jobs) :
    ]
    tail_ref[...] = bufs[0][2 * CHIP :, :E]
    core = lax.axis_index("core")
    loads = [
        pltpu.make_async_copy(s, t, sems.at[i])
        for i, (s, t) in enumerate(((kd_hbm, kd_ref), (q_hbm, q_ref), (w_hbm, w_ref)))
    ]
    for c in loads:
        c.start()
    for j, (mine, d) in enumerate(jobs):
        src, half = (mine_ref, core) if mine else (their_ref, 1 - core)
        multiply(mine, d, x_ref, bufs[2 * j], bufs[2 * j + 1], src, acc.at[half])
    loads[0].wait()
    states = [None] * 8
    for b in range(4):
        rows = slice(b * SPAN, (b + 1) * SPAN)
        for h in range(8):
            lanes = slice(h * E, (h + 1) * E)
            part = slice((h % 4) * E, (h % 4 + 1) * E)
            v = acc[h // 4, rows, part].astype(bf16)
            v_ref[rows, lanes] = v
            state = states[h]
            if b > 0:
                state = state * dec[32 + b : 33 + b, :]
                high = state.astype(bf16)
                st_ref[h, b - 1, :, :E] = high
                st_ref[h, b - 1, :, E:] = (state - high.astype(f32)).astype(bf16)
            update = dot(kd_ref[h, b], v)
            at = b * 8 + h
            states[h] = update if b == 0 else dec[at : at + 1, :] * state + update
    for h in range(4):
        part = slice(h * E, (h + 1) * E)
        keep_ref[part, :] = jnp.where(core == 0, states[h], states[h + 4])
        give_ref[part, :] = jnp.where(core == 0, states[h + 4], states[h])
    for c in loads[1:]:
        c.wait()


def post(jobs, dec, q, kd, w, mine, theirs, x, bufs):
    return pl.pallas_call(
        functools.partial(post_kernel, jobs),
        in_specs=[VM, HB, HB, HB] + [VM] * (3 + len(bufs)),
        out_specs=[VM] * 7,
        out_shape=[
            pltpu.VMEM((1024, 1024), bf16),
            pltpu.VMEM((HALF, E), f32),
            pltpu.VMEM((HALF, E), f32),
            pltpu.VMEM((64, E), bf16),
            pltpu.VMEM((8, 3, E, 2 * E), bf16),
            pltpu.VMEM((1024, 1024), bf16),
            pltpu.VMEM((8, 4, SPAN, SPAN), bf16),
        ],
        scratch_shapes=[
            pltpu.VMEM((2, 1024, HALF), f32),
            pltpu.VMEM((8, 4, E, SPAN), bf16),
            pltpu.SemaphoreType.DMA((3,)),
        ],
        compiler_params=params(10),
        name="post",
    )(dec, hbm(q), hbm(kd), hbm(w), mine, theirs, x, *bufs)


def within_kernel(ld_ref, v_ref, st_ref, q_ref, w_ref, comb_ref):
    half = SPAN // 2
    for b in range(4):
        rows = slice(b * SPAN, (b + 1) * SPAN)
        col = head_col(ld_ref[:, rows])
        for h in range(8):
            lanes = slice(h * E, (h + 1) * E)
            v = v_ref[rows, lanes]
            top = dot(w_ref[h, b, :half, :half], v[:half])
            low = dot(w_ref[h, b, half:, :], v)
            inner = jnp.concatenate([top, low], axis=0)
            if b > 0:
                o = dot(q_ref[rows, lanes], st_ref[h, b - 1])
                inner = inner + col[:, h : h + 1] * (o[:, :E] + o[:, E:])
            comb_ref[0, rows, lanes] = inner


def within(ld, v, st, q, w):
    return pl.pallas_call(
        within_kernel,
        in_specs=[VM] * 5,
        out_specs=VM,
        out_shape=pltpu.VMEM((ROOM, 1024, 1024), f32),
        compiler_params=params(6),
        cost_estimate=pl.CostEstimate(
            flops=3 * 10**9, transcendentals=0, bytes_accessed=10**7
        ),
        name="within",
    )(ld, v, st, q, w)


def weights_kernel(tails, tail, out_ref):
    x, z, core = lax.axis_index("x"), lax.axis_index("z"), lax.axis_index("core")
    first = core == 0
    rows, own = [], []
    for n in range(4):
        t = (tail[...] if n == 2 else tails[(0, 1, None, 2)[n]]).astype(f32)
        for e in range(4):
            f0 = t[16 * e : 16 * e + 1] + t[16 * e + 1 : 16 * e + 2] + t[16 * e + 2 : 16 * e + 3]
            at = 16 * e + 8
            f1 = t[at : at + 1] + t[at + 1 : at + 2] + t[at + 2 : at + 3]
            if not rows:
                own = [f0, f1]
            rows.append(f0 * f1)
    g = jnp.concatenate(rows, axis=0)
    n = lax.broadcasted_iota(jnp.int32, (16, E), 0)
    px = jnp.where(first, n // 4, n % 4)
    pz = jnp.where(first, n % 4, n // 4)
    k_at = ((x + 4 - px) % 4) * 4 + (z + 4 - pz) % 4
    out = []
    for d in range(4):
        tgt = jnp.where(first, lax.rem(x + d, 4) * 4 + z, x * 4 + lax.rem(z + d, 4))
        for e in range(4):
            src = jnp.where(
                first, x * 4 + lax.rem(z + 4 - e, 4), lax.rem(x + 4 - e, 4) * 4 + z
            )
            p = jnp.where((k_at > src) & (k_at < tgt), g, 1.0)
            p = p[:8] * p[8:]
            p = p[:4] * p[4:]
            p = p[:2] * p[2:]
            p = p[:1] * p[1:]
            out.append(jnp.where(src < tgt, p, 0.0))
    flat = jnp.concatenate(out + own + [jnp.zeros((E - 18, E), f32)], axis=0)
    turned = jnp.transpose(flat)
    out_ref[...] = jnp.where(first, turned[:8], jnp.concatenate([turned[4:8]] * 2, axis=0))


def weights(tails, tail):
    return pl.pallas_call(
        weights_kernel,
        in_specs=[VM] * 2,
        out_specs=VM,
        out_shape=pltpu.VMEM((8, E), f32),
        compiler_params=params(4),
        name="weights",
    )(tails, tail)


def one(ref, h, i):
    return jnp.broadcast_to(ref[h : h + 1, i : i + 1], (E, E))


def chip_kernel(wt, own_ref, recv_ref, f_ref, b_ref):
    first = lax.axis_index("core") == 0
    for h in range(4):
        r = slice(h * E, (h + 1) * E)
        a, b = own_ref[r, :], recv_ref[r, :]
        s = jnp.where(first, one(wt, h, 17) * a + b, a + one(wt, h, 16) * b)
        f_ref[r, :] = s
        b_ref[r, :] = s.astype(bf16)


def spread_kernel(wt, own_ref, r1, r2, r3, o0, o1, o2, o3):
    for h in range(4):
        r = slice(h * E, (h + 1) * E)
        src = [own_ref[r, :]] + [a[r, :].astype(f32) for a in (r1, r2, r3)]
        for d, o in enumerate((o0, o1, o2, o3)):
            s = None
            for e in range(4):
                t = one(wt, h, d * 4 + e) * src[e]
                s = t if s is None else s + t
            o[r, :] = s.astype(o.dtype)


def enter_kernel(wt, m0, r1, r2, r3, own_ref, recv_ref, mine_ref, other_ref):
    first = lax.axis_index("core") == 0
    for h in range(4):
        r = slice(h * E, (h + 1) * E)
        i = m0[r, :]
        for a in (r1, r2, r3):
            i = i + a[r, :].astype(f32)
        mine_ref[r, :] = jnp.where(first, i, one(wt, h, 17) * i + recv_ref[r, :])
        other_ref[r, :] = jnp.where(first, one(wt, h, 16) * i + own_ref[r, :], i)


def small(kernel, name, args, outs):
    return pl.pallas_call(
        kernel,
        in_specs=[VM] * len(args),
        out_specs=[VM] * len(outs),
        out_shape=[pltpu.VMEM((HALF, E), t) for t in outs],
        compiler_params=params(4),
        name=name,
    )(*args)


def outer_kernel(
    sf, ld_ref, mine_ref, other_ref, comb_ref, q_ref, out_ref, sq_ref
):
    first = lax.axis_index("core") == 0
    pairs = []
    for h in range(8):
        r = slice((h % 4) * E, (h % 4 + 1) * E)
        a, b = mine_ref[r, :], other_ref[r, :]
        m = jnp.where(first, a, b) if h < 4 else jnp.where(first, b, a)
        high = m.astype(bf16)
        pairs.append(jnp.concatenate([high, (m - high.astype(f32)).astype(bf16)], axis=1))
    for b in range(4):
        rows = slice(b * SPAN, (b + 1) * SPAN)
        col = head_col(ld_ref[:, rows]) * sf[b : b + 1, :8]
        total = None
        for h in range(8):
            lanes = slice(h * E, (h + 1) * E)
            q = q_ref[rows, lanes]
            o = dot(q, pairs[h])
            o = (o[:, :E] + o[:, E:]) * col[:, h : h + 1]
            o = comb_ref[0, rows, lanes] + o
            out_ref[rows, lanes] = o
            total = o * o if total is None else total + o * o
        for t in range(2):
            tt = jnp.transpose(total[t * E : (t + 1) * E, :])
            sq_ref[b * 2 + t : b * 2 + t + 1, :] = jnp.sum(tt, axis=0, keepdims=True)


def outer(sf, ld, q, mine, other, comb):
    return pl.pallas_call(
        outer_kernel,
        in_specs=[VM] * 6,
        out_specs=[VM, VM],
        out_shape=[pltpu.VMEM((1024, 1024), f32), pltpu.VMEM((8, E), f32)],
        compiler_params=params(6),
        name="outer",
    )(sf, ld, mine, other, comb, vmem(q))


def norm_kernel(out_ref, s0, s1, s2, s3, gain_ref, y_hbm, y_ref, sems):
    total = s0[...] + s1[...] + s2[...] + s3[...]
    scale = lax.rsqrt(total / (SHARD_ATTN_PARTS * E) + 1e-06)
    copies = []
    for t in range(8):
        col = jnp.transpose(jnp.broadcast_to(scale[t : t + 1, :], (E, E)))
        rows = slice(t * E, (t + 1) * E)
        for h in range(8):
            lanes = slice(h * E, (h + 1) * E)
            y_ref[rows, lanes] = (out_ref[rows, lanes] * col * gain_ref[:, lanes]).astype(bf16)
        c = pltpu.make_async_copy(y_ref.at[rows, :], y_hbm.at[rows, :], sems.at[t])
        c.start()
        copies.append(c)
    for c in copies:
        c.wait()


def norm(out, sqs, gain):
    return pl.pallas_call(
        norm_kernel,
        in_specs=[VM] * 6,
        out_specs=HB,
        out_shape=jax.ShapeDtypeStruct((1024, 1024), bf16),
        scratch_shapes=[pltpu.VMEM((1024, 1024), bf16), pltpu.SemaphoreType.DMA((8,))],
        compiler_params=params(8),
        name="norm",
    )(out, *sqs, gain)


def per_device(inputs, q, k, value_weight, ld, doc_start, gain):
    x, z, core = lax.axis_index("x"), lax.axis_index("z"), lax.axis_index("core")
    first = core == 0
    bar = lax.optimization_barrier

    fx, dec, sf = prep(doc_start, ld)
    my_w = lax.dynamic_slice(value_weight, (0, core * HALF), (CHIP // 2, HALF))
    their_w = lax.dynamic_slice(value_weight, (0, (1 - core) * HALF), (CHIP // 2, HALF))
    got = swap(jnp.concatenate([their_w, fx], axis=0))
    recv_w, recv_f = got[: CHIP // 2], got[CHIP // 2 :]
    chip_w = jnp.where(
        first,
        jnp.concatenate([my_w, recv_w], axis=0),
        jnp.concatenate([recv_w, my_w], axis=0),
    )
    chip_w = jnp.concatenate([chip_w, fx[:8], recv_f[:8]], axis=0)
    chip_w, ld, q, k = bar((chip_w, ld, q, k))
    line = [chip_w] + [crossed(chip_w, "z", "x", d, d) for d in (1, 2, 3)]
    w, kd, xv = pre(ld, q, k, inputs)
    line, w = bar((tuple(line), w))
    p_lo = jnp.concatenate([a[:CHIP] for a in line[:2]] + [a[CHIP:] for a in line], axis=0)
    p_hi = jnp.concatenate([a[:CHIP] for a in line[2:]], axis=0)
    up_lo = crossed(p_lo, "x", "z", 1, 1)
    dn_hi = crossed(p_hi, "x", "z", -1, -1)
    up_hi = crossed(p_hi, "x", "z", 1, 1)
    dn_lo = crossed(p_lo, "x", "z", -1, -1)
    sums = mm(((True, 0), (False, 0)), xv, (p_lo, p_hi, swap(p_lo), swap(p_hi)), False)[0]
    up_lo, dn_hi, sums = bar((up_lo, dn_hi, sums))
    op_lo = crossed(up_lo, "x", "z", 1, 1)
    op_hi = crossed(dn_hi, "x", "z", -1, -1)
    bufs = (up_lo, up_hi, dn_lo, dn_hi)
    mine = mm(((True, 1), (True, 3)), xv, bufs, False, 0, sums)[0]
    bufs = tuple(swap(a) for a in bufs)
    op_lo, op_hi, mine = bar((op_lo, op_hi, mine))
    theirs, = mm(((False, 1), (False, 3)), xv, bufs, False, 1, sums)
    tails = jnp.stack([a[2 * CHIP :, :E] for a in (p_lo, up_lo, dn_lo)])
    bufs = [op_lo, op_hi, swap(op_lo), swap(op_hi)]
    theirs, tails = bar((theirs, tails))
    v, own, give, tail, st, qv, wv = post(
        ((True, 2), (False, 2)), vmem(dec), q, kd, w, mine, theirs, xv, [vmem(a) for a in bufs]
    )
    recv = vmem(swap(give))
    wt = weights(tails, tail)
    chip, chip16 = small(chip_kernel, "chip", (wt, own, recv), (f32, bf16))
    got = [vmem(crossed(chip16, "z", "x", d, d)) for d in (1, 2, 3)]
    v, chip = bar((v, chip))
    comb = within(ld, v, st, qv, wv)
    *got, comb = bar((*got, comb))
    sent = small(spread_kernel, "spread", (wt, chip, *got), (f32, bf16, bf16, bf16))
    got = [vmem(crossed(sent[d], "x", "z", d, d)) for d in (1, 2, 3)]
    mine, give = small(enter_kernel, "enter", (wt, sent[0], *got, own, recv), (f32, f32))
    other = vmem(swap(give))
    out, sq = outer(vmem(sf), ld, q, mine, other, comb)
    sqs = [sq] + [vmem(ring(sq, "head", d)) for d in (1, 2, 3)]
    return norm(out, sqs, gain.reshape(1, -1))


def solution(mesh):
    mesh = Mesh(mesh.devices.reshape(4, 4, 2, 4), ("x", "z", "core", "head"))
    placed = (
        P(SEQ, None),
        P(SEQ, "head"),
        P(SEQ, "head"),
        P(SEQ, "head"),
        P("head", SEQ),
        P(SEQ),
        P("head"),
    )
    return jax.shard_map(
        per_device, mesh=mesh, in_specs=placed, out_specs=P(SEQ, "head"), check_vma=False
    )
```

```python
import functools
import jax
import jax.numpy as jnp
from jax import lax
from jax.experimental import pallas as pl
from jax.experimental.pallas import tpu as pltpu
from jax.sharding import Mesh, PartitionSpec as P

SHARD_ATTN_PARTS = 32
E = 128
SPAN = 256
SEQ = ("x", "z", "core")
SWAP = [(0, 1), (1, 0)]
VM = pl.BlockSpec(memory_space=pltpu.VMEM)
HB = pl.BlockSpec(memory_space=pltpu.HBM)
MIB = 1024 * 1024
HALF = 512
LINE = 1536
CHIP = 384
ROOM = 2
ROOM_P = 4
f32, bf16 = jnp.float32, jnp.bfloat16


def swap(a):
    return lax.ppermute(a, "core", SWAP)


def ring(a, axis, step):
    return lax.ppermute(a, axis, [(i, (i + step) % 4) for i in range(4)])


def crossed(a, first, second, step0, step1):
    pairs = []
    for x in range(4):
        for z in range(4):
            for c in range(2):
                axis, step = ((first, step0), (second, step1))[c]
                tx = (x + step) % 4 if axis == "x" else x
                tz = (z + step) % 4 if axis == "z" else z
                pairs.append((x * 8 + z * 2 + c, tx * 8 + tz * 2 + c))
    return lax.ppermute(a, SEQ, pairs)


def dot(a, b, dims=((1,), (0,))):
    return lax.dot_general(a, b, (dims, ((), ())), preferred_element_type=f32)


def block_cum(ld):
    lane = lax.broadcasted_iota(jnp.int32, ld.shape, 1)
    step = 1
    while step < SPAN:
        ld = ld + jnp.where(lane >= step, pltpu.roll(ld, step, 1), 0.0)
        step *= 2
    return ld


def vmem(a):
    return pltpu.with_memory_space_constraint(a, pltpu.VMEM)


def hbm(a):
    return pltpu.with_memory_space_constraint(a, pltpu.HBM)


def params(mib):
    return pltpu.CompilerParams(vmem_limit_bytes=mib * MIB)


def prep_kernel(doc, ld_ref, fx_ref, dec_ref, sf_ref):
    lane = lax.broadcasted_iota(jnp.int32, (E, E), 1)
    mat = jnp.zeros((E, E), f32)
    place = lax.broadcasted_iota(jnp.int32, (8, E), 1)
    start = jnp.ones((8, E), f32)
    starts = jnp.zeros((8, E), f32)
    surv = []
    for b in range(4):
        total = jnp.sum(ld_ref[:, b * SPAN : (b + 1) * SPAN], axis=1, keepdims=True)
        decay = jnp.broadcast_to(jnp.exp(total), (8, E))
        dec_ref[b * 8 : b * 8 + 8, :] = decay
        tall = jnp.concatenate([decay, jnp.zeros((E - 8, E), f32)], axis=0)
        mat = jnp.where(lane == b, tall, mat)
        surv.append(1.0 - jnp.full((1, E), doc[b], jnp.int32).astype(f32))
        start = start * surv[b]
        starts = jnp.where(place == b, start, starts)
        start = start * decay
    dec_ref[32:40, :] = jnp.concatenate(surv + [jnp.zeros((4, E), f32)], axis=0)
    rows = jnp.transpose(mat)
    f = None
    for b in range(4):
        f = surv[b] if b == 0 else f * surv[b]
        f = f * rows[b : b + 1, :]
    sf_ref[...] = starts
    high = f.astype(bf16).astype(f32)
    mid = (f - high).astype(bf16).astype(f32)
    low = f - high - mid
    tile = jnp.concatenate([high, mid, low, jnp.zeros((13, E), f32)], axis=0)
    fx_ref[:, E:] = jnp.zeros((16, HALF - E), bf16)
    fx_ref[:, :E] = tile.astype(bf16)


def prep(doc, ld):
    return pl.pallas_call(
        prep_kernel,
        in_specs=[pl.BlockSpec(memory_space=pltpu.SMEM), VM],
        out_specs=[VM] * 3,
        out_shape=[
            pltpu.VMEM((16, HALF), bf16),
            jax.ShapeDtypeStruct((40, E), f32),
            jax.ShapeDtypeStruct((8, E), f32),
        ],
        compiler_params=params(4),
        name="prep",
    )(doc, ld)


def pre_kernel(
    ld_ref, q_hbm, k_hbm, x_hbm, w_hbm, kd_hbm, x_ref, q_ref, k_ref, w_ref, kd_ref, sems, xsems
):
    half = SPAN // 2
    low = lax.broadcasted_iota(jnp.int32, (half, half), 0) >= lax.broadcasted_iota(
        jnp.int32, (half, half), 1
    )

    def loads(h):
        lanes = pl.ds(pl.multiple_of(h * E, E), E)
        return (
            pltpu.make_async_copy(q_hbm.at[:, lanes], q_ref.at[:, lanes], sems.at[0, h]),
            pltpu.make_async_copy(k_hbm.at[:, lanes], k_ref.at[:, lanes], sems.at[1, h]),
        )

    def stores(h):
        return (
            pltpu.make_async_copy(w_ref.at[h], w_hbm.at[h], sems.at[2, h]),
            pltpu.make_async_copy(kd_ref.at[h], kd_hbm.at[h], sems.at[3, h]),
        )

    for h in range(8):
        for c in loads(h):
            c.start()
    inputs = []
    for r in range(8):
        rows = slice(r * E, (r + 1) * E)
        inputs.append(
            pltpu.make_async_copy(x_hbm.at[rows, :], x_ref.at[rows, :], xsems.at[r])
        )
        inputs[r].start()
    w_ref[:, :, :half, half:] = jnp.zeros((8, 4, half, half), bf16)
    cums = [block_cum(ld_ref[:, b * SPAN : (b + 1) * SPAN]) for b in range(4)]

    def one_head(h, carry):
        for c in loads(h):
            c.wait()
        head = lax.broadcasted_iota(jnp.int32, (8, SPAN), 0) == h
        lanes = pl.ds(pl.multiple_of(h * E, E), E)
        for b in range(4):
            row = jnp.sum(jnp.where(head, cums[b], 0.0), axis=0, keepdims=True)
            col = jnp.transpose(jnp.broadcast_to(row, (8, SPAN)))[:, 0:1]
            last = row[:, SPAN - 1 : SPAN]
            rows = slice(b * SPAN, (b + 1) * SPAN)
            k = k_ref[rows, lanes]
            kt = jnp.transpose(k.astype(f32))
            kd_ref[h, b] = (kt * jnp.exp(last - row)).astype(bf16)
            q = q_ref[rows, lanes]
            s = dot(q[:half], k[:half], ((1,), (1,)))
            g = jnp.exp(jnp.where(low, col[:half] - row[:, :half], -1e30))
            w_ref[h, b, :half, :half] = (s * g).astype(bf16)
            s = dot(q[half:], k, ((1,), (1,)))
            g = jnp.exp(col[half:] - row[:, :half])
            w_ref[h, b, half:, :half] = (s[:, :half] * g).astype(bf16)
            g = jnp.exp(jnp.where(low, col[half:] - row[:, half:], -1e30))
            w_ref[h, b, half:, half:] = (s[:, half:] * g).astype(bf16)
        for c in stores(h):
            c.start()
        return carry

    lax.fori_loop(0, 8, one_head, 0)
    for h in range(8):
        for c in stores(h):
            c.wait()
    for c in inputs:
        c.wait()


def pre(ld, q, k, x):
    shapes = ((8, 4, SPAN, SPAN), (8, 4, E, SPAN))
    return pl.pallas_call(
        pre_kernel,
        in_specs=[VM, HB, HB, HB],
        out_specs=[HB, HB, VM],
        out_shape=[pltpu.HBM(s, bf16) for s in shapes] + [pltpu.VMEM(x.shape, bf16)],
        scratch_shapes=[pltpu.VMEM((1024, 1024), bf16)] * 2
        + [pltpu.VMEM(s, bf16) for s in shapes]
        + [pltpu.SemaphoreType.DMA((4, 8)), pltpu.SemaphoreType.DMA((8,))],
        compiler_params=params(14),
        cost_estimate=pl.CostEstimate(flops=10**9, transcendentals=2 * 10**6, bytes_accessed=10**7),
        name="pre",
    )(ld, hbm(q), hbm(k), hbm(x))


def multiply(mine, d, x_ref, lo, hi, src, dst):
    x, z, core = lax.axis_index("x"), lax.axis_index("z"), lax.axis_index("core")
    first = (core == 0) if mine else (core == 1)
    line = lax.rem(jnp.where(first, x, z) + 4 - d, 4)
    spans = []
    for e in range(4):
        other = lax.rem(jnp.where(first, z, x) + 4 - e, 4)
        at = jnp.where(first, line * LINE + other * CHIP, other * LINE + line * CHIP)
        spans.append(pl.ds(pl.multiple_of(at, 128), CHIP))
    for r in range(2):
        rows = slice(r * 512, (r + 1) * 512)
        part = src[rows, :] if src is not None else None
        for w, (s0, s1) in ((lo, spans[:2]), (hi, spans[2:])):
            lhs = jnp.concatenate([x_ref[rows, s0], x_ref[rows, s1]], axis=1)
            p = dot(lhs, w[: 2 * CHIP, :])
            part = p if part is None else part + p
        dst[rows, :] = part


def mm_kernel(jobs, plane, here, x_ref, *refs):
    n = 2 * len(jobs)
    bufs, refs = refs[:n], refs[n:]
    src = None
    if plane is not None:
        src = refs[0] if plane < 0 else refs[0].at[plane]
        refs = refs[1:]
    out, tails = refs[:2]
    copies = []
    if here:
        wv = bufs
        for j in range(len(jobs)):
            tails[j] = bufs[2 * j][2 * CHIP :, :E]
    else:
        wv, sems = refs[2:]
        for i, b in enumerate(bufs):
            copies.append(
                pltpu.make_async_copy(b.at[: 2 * CHIP, :], wv.at[i], sems.at[i])
            )
        wv = [wv.at[i] for i in range(n)]
        for j in range(len(jobs)):
            copies.append(
                pltpu.make_async_copy(
                    bufs[2 * j].at[2 * CHIP :, :E], tails.at[j], sems.at[n + j]
                )
            )
    for c in copies:
        c.start()
    for j, (mine, d) in enumerate(jobs):
        for c in copies[2 * j : 2 * j + 2]:
            c.wait()
        if plane is None:
            dst, before = out.at[j], None
        else:
            dst, before = out, (out if j else src)
        multiply(mine, d, x_ref, wv[2 * j], wv[2 * j + 1], before, dst)
    for c in copies[n:]:
        c.wait()


def mm(jobs, x, bufs, plane=None, before=None, here=False):
    n = 2 * len(jobs)
    extra = [] if before is None else [before]
    scratch = [] if here else [
        pltpu.VMEM((n, 2 * CHIP, HALF), bf16),
        pltpu.SemaphoreType.DMA((n + len(jobs),)),
    ]
    return pl.pallas_call(
        functools.partial(mm_kernel, jobs, plane, here),
        in_specs=[VM] + [VM if here else HB] * n + [VM] * len(extra),
        out_specs=[VM] * 2,
        out_shape=[
            pltpu.VMEM((ROOM_P, 1024, HALF) if plane is None else (1024, HALF), f32),
            pltpu.VMEM((len(jobs), 64, E), bf16),
        ],
        scratch_shapes=scratch,
        compiler_params=params(6 if here else 10),
        cost_estimate=pl.CostEstimate(
            flops=1024 * LINE * HALF * n, transcendentals=0, bytes_accessed=n * 5 * 10**6
        ),
        name="project",
    )(x, *[(vmem if here else hbm)(a) for a in bufs], *extra)


def head_col(ld_block):
    return jnp.transpose(jnp.exp(block_cum(ld_block)))


def post_kernel(jobs, dec, q_hbm, kd_hbm, w_hbm, mine_ref, their_ref, x_ref, *refs):
    bufs = refs[: 2 * len(jobs)]
    v_ref, keep_ref, give_ref, tail_ref, st_ref, q_ref, w_ref, acc, kd_ref, sems = refs[
        2 * len(jobs) :
    ]
    tail_ref[0] = bufs[0][2 * CHIP :, :E]
    tail_ref[1] = bufs[2][2 * CHIP :, :E]
    core = lax.axis_index("core")
    loads = [
        pltpu.make_async_copy(s, t, sems.at[i])
        for i, (s, t) in enumerate(((kd_hbm, kd_ref), (q_hbm, q_ref), (w_hbm, w_ref)))
    ]
    for c in loads:
        c.start()
    for j, (mine, d) in enumerate(jobs):
        src, half = (mine_ref, core) if mine else (their_ref, 1 - core)
        multiply(mine, d, x_ref, bufs[2 * j], bufs[2 * j + 1], src, acc.at[half])
    loads[0].wait()
    states = [None] * 8
    for b in range(4):
        rows = slice(b * SPAN, (b + 1) * SPAN)
        for h in range(8):
            lanes = slice(h * E, (h + 1) * E)
            part = slice((h % 4) * E, (h % 4 + 1) * E)
            v = acc[h // 4, rows, part].astype(bf16)
            v_ref[rows, lanes] = v
            state = states[h]
            if b > 0:
                state = state * dec[32 + b : 33 + b, :]
                high = state.astype(bf16)
                st_ref[h, b - 1, :, :E] = high
                st_ref[h, b - 1, :, E:] = (state - high.astype(f32)).astype(bf16)
            update = dot(kd_ref[h, b], v)
            at = b * 8 + h
            states[h] = update if b == 0 else dec[at : at + 1, :] * state + update
    for h in range(4):
        part = slice(h * E, (h + 1) * E)
        keep_ref[part, :] = jnp.where(core == 0, states[h], states[h + 4])
        give_ref[part, :] = jnp.where(core == 0, states[h + 4], states[h])
    for c in loads[1:]:
        c.wait()


def post(jobs, dec, q, kd, w, mine, theirs, x, bufs):
    return pl.pallas_call(
        functools.partial(post_kernel, jobs),
        in_specs=[VM, HB, HB, HB] + [VM] * (3 + len(bufs)),
        out_specs=[VM] * 7,
        out_shape=[
            pltpu.VMEM((1024, 1024), bf16),
            pltpu.VMEM((HALF, E), f32),
            pltpu.VMEM((HALF, E), f32),
            pltpu.VMEM((2, 64, E), bf16),
            pltpu.VMEM((8, 3, E, 2 * E), bf16),
            pltpu.VMEM((1024, 1024), bf16),
            pltpu.VMEM((8, 4, SPAN, SPAN), bf16),
        ],
        scratch_shapes=[
            pltpu.VMEM((2, 1024, HALF), f32),
            pltpu.VMEM((8, 4, E, SPAN), bf16),
            pltpu.SemaphoreType.DMA((3,)),
        ],
        compiler_params=params(10),
        name="post",
    )(dec, hbm(q), hbm(kd), hbm(w), mine, theirs, x, *bufs)


def within_kernel(ld_ref, v_ref, st_ref, q_ref, w_ref, comb_ref):
    half = SPAN // 2
    for b in range(4):
        rows = slice(b * SPAN, (b + 1) * SPAN)
        col = head_col(ld_ref[:, rows])
        for h in range(8):
            lanes = slice(h * E, (h + 1) * E)
            v = v_ref[rows, lanes]
            top = dot(w_ref[h, b, :half, :half], v[:half])
            low = dot(w_ref[h, b, half:, :], v)
            inner = jnp.concatenate([top, low], axis=0)
            if b > 0:
                o = dot(q_ref[rows, lanes], st_ref[h, b - 1])
                inner = inner + col[:, h : h + 1] * (o[:, :E] + o[:, E:])
            comb_ref[0, rows, lanes] = inner


def within(ld, v, st, q, w):
    return pl.pallas_call(
        within_kernel,
        in_specs=[VM] * 5,
        out_specs=VM,
        out_shape=pltpu.VMEM((ROOM, 1024, 1024), f32),
        compiler_params=params(6),
        cost_estimate=pl.CostEstimate(
            flops=3 * 10**9, transcendentals=0, bytes_accessed=10**7
        ),
        name="within",
    )(ld, v, st, q, w)


def weights_kernel(t_own, t_mine, t_up, t_dn, t_last, out_ref):
    x, z, core = lax.axis_index("x"), lax.axis_index("z"), lax.axis_index("core")
    first = core == 0

    def factors(tiles):
        out = []
        for t in tiles:
            t = t.astype(f32)
            for e in range(4):
                r = [t[16 * e + i : 16 * e + i + 1] for i in range(3)]
                out.append(r[0] + r[1] + r[2])
        return out

    near = factors((t_own[0], t_mine[0], t_last[0], t_mine[1]))
    far = factors((t_own[1], t_up[0], t_last[1], t_dn[0]))
    own = [near[0], far[0]]
    rows = [near[4 * n + e] * far[4 * e + n] for n in range(4) for e in range(4)]
    g = jnp.concatenate(rows, axis=0)
    n = lax.broadcasted_iota(jnp.int32, (16, E), 0)
    px = jnp.where(first, n // 4, n % 4)
    pz = jnp.where(first, n % 4, n // 4)
    k_at = ((x + 4 - px) % 4) * 4 + (z + 4 - pz) % 4
    out = []
    for d in range(4):
        tgt = jnp.where(first, lax.rem(x + d, 4) * 4 + z, x * 4 + lax.rem(z + d, 4))
        for e in range(4):
            src = jnp.where(
                first, x * 4 + lax.rem(z + 4 - e, 4), lax.rem(x + 4 - e, 4) * 4 + z
            )
            p = jnp.where((k_at > src) & (k_at < tgt), g, 1.0)
            p = p[:8] * p[8:]
            p = p[:4] * p[4:]
            p = p[:2] * p[2:]
            p = p[:1] * p[1:]
            out.append(jnp.where(src < tgt, p, 0.0))
    flat = jnp.concatenate(out + own + [jnp.zeros((E - 18, E), f32)], axis=0)
    turned = jnp.transpose(flat)
    out_ref[...] = jnp.where(first, turned[:8], jnp.concatenate([turned[4:8]] * 2, axis=0))


def weights(*tails):
    return pl.pallas_call(
        weights_kernel,
        in_specs=[VM] * 5,
        out_specs=VM,
        out_shape=pltpu.VMEM((8, E), f32),
        compiler_params=params(4),
        name="weights",
    )(*tails)


def one(ref, h, i):
    return jnp.broadcast_to(ref[h : h + 1, i : i + 1], (E, E))


def chip_kernel(wt, own_ref, recv_ref, f_ref, b_ref):
    first = lax.axis_index("core") == 0
    for h in range(4):
        r = slice(h * E, (h + 1) * E)
        a, b = own_ref[r, :], recv_ref[r, :]
        s = jnp.where(first, one(wt, h, 17) * a + b, a + one(wt, h, 16) * b)
        f_ref[r, :] = s
        b_ref[r, :] = s.astype(bf16)


def spread_kernel(wt, own_ref, r1, r2, r3, o0, o1, o2, o3):
    for h in range(4):
        r = slice(h * E, (h + 1) * E)
        src = [own_ref[r, :]] + [a[r, :].astype(f32) for a in (r1, r2, r3)]
        for d, o in enumerate((o0, o1, o2, o3)):
            s = None
            for e in range(4):
                t = one(wt, h, d * 4 + e) * src[e]
                s = t if s is None else s + t
            o[r, :] = s.astype(o.dtype)


def enter_kernel(wt, m0, r1, r2, r3, own_ref, recv_ref, mine_ref, other_ref):
    first = lax.axis_index("core") == 0
    for h in range(4):
        r = slice(h * E, (h + 1) * E)
        i = m0[r, :]
        for a in (r1, r2, r3):
            i = i + a[r, :].astype(f32)
        mine_ref[r, :] = jnp.where(first, i, one(wt, h, 17) * i + recv_ref[r, :])
        other_ref[r, :] = jnp.where(first, one(wt, h, 16) * i + own_ref[r, :], i)


def small(kernel, name, args, outs):
    return pl.pallas_call(
        kernel,
        in_specs=[VM] * len(args),
        out_specs=[VM] * len(outs),
        out_shape=[pltpu.VMEM((HALF, E), t) for t in outs],
        compiler_params=params(4),
        name=name,
    )(*args)


def outer_kernel(side, sf, ld_ref, state_ref, comb_ref, q_ref, *refs):
    before, (out_ref, sq_ref) = refs[:-2], refs[-2:]
    core = lax.axis_index("core")
    half = core if side == 0 else 1 - core
    pairs = []
    for h in range(4):
        m = state_ref[h * E : (h + 1) * E, :]
        high = m.astype(bf16)
        pairs.append(jnp.concatenate([high, (m - high.astype(f32)).astype(bf16)], axis=1))
    for b in range(4):
        rows = slice(b * SPAN, (b + 1) * SPAN)
        scale = jnp.exp(block_cum(ld_ref[:, rows])) * sf[:, b : b + 1]
        scale = jnp.where(half == 0, scale[:4], scale[4:])
        col = jnp.transpose(jnp.concatenate([scale, scale], axis=0))
        total = None
        for h in range(4):
            lanes = pl.ds(pl.multiple_of(half * HALF + h * E, E), E)
            o = dot(q_ref[rows, lanes], pairs[h])
            o = (o[:, :E] + o[:, E:]) * col[:, h : h + 1]
            o = comb_ref[0, rows, lanes] + o
            out_ref[rows, h * E : (h + 1) * E] = o
            total = o * o if total is None else total + o * o
        for t in range(2):
            tt = jnp.transpose(total[t * E : (t + 1) * E, :])
            r = slice(b * 2 + t, b * 2 + t + 1)
            sq = jnp.sum(tt, axis=0, keepdims=True)
            sq_ref[r, :] = sq + before[0][r, :] if before else sq


def outer(side, sf, ld, state, comb, q, *before):
    return pl.pallas_call(
        functools.partial(outer_kernel, side),
        in_specs=[VM] * (5 + len(before)),
        out_specs=[VM, VM],
        out_shape=[pltpu.VMEM((1024, HALF), f32), pltpu.VMEM((8, E), f32)],
        compiler_params=params(6),
        cost_estimate=pl.CostEstimate(
            flops=6 * 10**8, transcendentals=0, bytes_accessed=6 * 10**6
        ),
        name="outer",
    )(sf, ld, state, comb, q, *before)


def norm_kernel(mine_ref, other_ref, s0, s1, s2, s3, gain_ref, y_hbm, y_ref, sems):
    core = lax.axis_index("core")
    total = s0[...] + s1[...] + s2[...] + s3[...]
    scale = lax.rsqrt(total / (SHARD_ATTN_PARTS * E) + 1e-06)
    copies = []
    for t in range(8):
        col = jnp.transpose(jnp.broadcast_to(scale[t : t + 1, :], (E, E)))
        rows = slice(t * E, (t + 1) * E)
        for ref, half in ((mine_ref, core), (other_ref, 1 - core)):
            for h in range(4):
                lanes = pl.ds(pl.multiple_of(half * HALF + h * E, E), E)
                y = ref[rows, h * E : (h + 1) * E] * col * gain_ref[:, lanes]
                y_ref[rows, lanes] = y.astype(bf16)
        c = pltpu.make_async_copy(y_ref.at[rows, :], y_hbm.at[rows, :], sems.at[t])
        c.start()
        copies.append(c)
    for c in copies:
        c.wait()


def norm(mine, other, sqs, gain):
    return pl.pallas_call(
        norm_kernel,
        in_specs=[VM] * 7,
        out_specs=HB,
        out_shape=jax.ShapeDtypeStruct((1024, 1024), bf16),
        scratch_shapes=[pltpu.VMEM((1024, 1024), bf16), pltpu.SemaphoreType.DMA((8,))],
        compiler_params=params(8),
        name="norm",
    )(mine, other, *sqs, gain)


def per_device(inputs, q, k, value_weight, ld, doc_start, gain):
    x, z, core = lax.axis_index("x"), lax.axis_index("z"), lax.axis_index("core")
    first = core == 0
    bar = lax.optimization_barrier

    my_w = lax.dynamic_slice(value_weight, (0, core * HALF), (CHIP // 2, HALF))
    their_w = lax.dynamic_slice(value_weight, (0, (1 - core) * HALF), (CHIP // 2, HALF))
    recv_w = swap(their_w)
    fx, dec, sf = prep(doc_start, ld)
    chip_w = jnp.where(
        first,
        jnp.concatenate([my_w, recv_w, fx], axis=0),
        jnp.concatenate([recv_w, my_w, fx], axis=0),
    )
    chip_w, ld, q, k = bar((chip_w, ld, q, k))
    line = [chip_w] + [crossed(chip_w, "z", "x", d, d) for d in (1, 2, 3)]
    w, kd, xv = pre(ld, q, k, inputs)
    line, w = bar((tuple(line), w))
    p_lo = jnp.concatenate([a[:CHIP] for a in line[:2]] + [a[CHIP:] for a in line], axis=0)
    p_hi = jnp.concatenate([a[:CHIP] for a in line[2:]], axis=0)
    up_lo = crossed(p_lo, "x", "z", 1, 1)
    dn_hi = crossed(p_hi, "x", "z", -1, -1)
    up_hi = crossed(p_hi, "x", "z", 1, 1)
    dn_lo = crossed(p_lo, "x", "z", -1, -1)
    bufs = (p_lo, p_hi, swap(p_lo), swap(p_hi))
    sums, t_own = mm(((True, 0), (False, 0)), xv, bufs, here=True)
    up_lo, dn_hi, sums = bar((up_lo, dn_hi, sums))
    op_lo = crossed(up_lo, "x", "z", 1, 1)
    op_hi = crossed(dn_hi, "x", "z", -1, -1)
    up_lo, up_hi, dn_lo, dn_hi = bar((up_lo, up_hi, dn_lo, dn_hi))
    swapped = (swap(up_lo), swap(up_hi))
    bufs = (up_lo, up_hi, dn_lo, dn_hi)
    mine, t_mine = mm(((True, 1), (True, 3)), xv, bufs, 0, sums, True)
    op_lo, op_hi, dn_lo, dn_hi, mine = bar((op_lo, op_hi, dn_lo, dn_hi, mine))
    theirs, t_up = mm(((False, 1),), xv, swapped, 1, sums, True)
    theirs, t_dn = mm(((False, 3),), xv, (swap(dn_lo), swap(dn_hi)), -1, theirs, True)
    bufs = [op_lo, op_hi, swap(op_lo), swap(op_hi)]
    v, own, give, t_last, st, qv, wv = post(
        ((True, 2), (False, 2)), vmem(dec), q, kd, w, mine, theirs, xv, [vmem(a) for a in bufs]
    )
    recv = vmem(swap(give))
    wt = weights(t_own, t_mine, t_up, t_dn, t_last)
    chip, chip16 = small(chip_kernel, "chip", (wt, own, recv), (f32, bf16))
    got = [vmem(crossed(chip16, "z", "x", d, d)) for d in (1, 2, 3)]
    v, chip = bar((v, chip))
    comb = within(ld, v, st, qv, wv)
    *got, comb = bar((*got, comb))
    sent = small(spread_kernel, "spread", (wt, chip, *got), (f32, bf16, bf16, bf16))
    got = [vmem(crossed(sent[d], "x", "z", d, d)) for d in (1, 2, 3)]
    state, give = small(enter_kernel, "enter", (wt, sent[0], *got, own, recv), (f32, f32))
    sf, qv = vmem(sf), vmem(q)
    mine, sq = outer(0, sf, ld, state, comb, qv)
    other, sq = outer(1, sf, ld, vmem(swap(give)), comb, qv, sq)
    sqs = [sq] + [vmem(ring(sq, "head", d)) for d in (1, 2, 3)]
    return norm(mine, other, sqs, gain.reshape(1, -1))


def solution(mesh):
    mesh = Mesh(mesh.devices.reshape(4, 4, 2, 4), ("x", "z", "core", "head"))
    placed = (
        P(SEQ, None),
        P(SEQ, "head"),
        P(SEQ, "head"),
        P(SEQ, "head"),
        P("head", SEQ),
        P(SEQ),
        P("head"),
    )
    return jax.shard_map(
        per_device, mesh=mesh, in_specs=placed, out_specs=P(SEQ, "head"), check_vma=False
    )
```

```python
import functools
import jax
import jax.numpy as jnp
from jax import lax
from jax.experimental import pallas as pl
from jax.experimental.pallas import tpu as pltpu
from jax.sharding import Mesh, PartitionSpec as P

SHARD_ATTN_PARTS = 32
E = 128
SPAN = 256
SEQ = ("x", "z", "core")
SWAP = [(0, 1), (1, 0)]
VM = pl.BlockSpec(memory_space=pltpu.VMEM)
HB = pl.BlockSpec(memory_space=pltpu.HBM)
MIB = 1024 * 1024
HALF = 512
LINE = 1536
CHIP = 384
ROOM = 2
ROOM_P = 4
f32, bf16 = jnp.float32, jnp.bfloat16


def swap(a):
    return lax.ppermute(a, "core", SWAP)


def ring(a, axis, step):
    return lax.ppermute(a, axis, [(i, (i + step) % 4) for i in range(4)])


def crossed(a, first, second, step0, step1):
    pairs = []
    for x in range(4):
        for z in range(4):
            for c in range(2):
                axis, step = ((first, step0), (second, step1))[c]
                tx = (x + step) % 4 if axis == "x" else x
                tz = (z + step) % 4 if axis == "z" else z
                pairs.append((x * 8 + z * 2 + c, tx * 8 + tz * 2 + c))
    return lax.ppermute(a, SEQ, pairs)


def dot(a, b, dims=((1,), (0,))):
    return lax.dot_general(a, b, (dims, ((), ())), preferred_element_type=f32)


def block_cum(ld):
    lane = lax.broadcasted_iota(jnp.int32, ld.shape, 1)
    step = 1
    while step < SPAN:
        ld = ld + jnp.where(lane >= step, pltpu.roll(ld, step, 1), 0.0)
        step *= 2
    return ld


def vmem(a):
    return pltpu.with_memory_space_constraint(a, pltpu.VMEM)


def hbm(a):
    return pltpu.with_memory_space_constraint(a, pltpu.HBM)


def params(mib):
    return pltpu.CompilerParams(vmem_limit_bytes=mib * MIB)


def prep_kernel(doc, ld_ref, fx_ref, dec_ref, sf_ref):
    lane = lax.broadcasted_iota(jnp.int32, (E, E), 1)
    mat = jnp.zeros((E, E), f32)
    place = lax.broadcasted_iota(jnp.int32, (8, E), 1)
    start = jnp.ones((8, E), f32)
    starts = jnp.zeros((8, E), f32)
    surv = []
    for b in range(4):
        total = jnp.sum(ld_ref[:, b * SPAN : (b + 1) * SPAN], axis=1, keepdims=True)
        decay = jnp.broadcast_to(jnp.exp(total), (8, E))
        dec_ref[b * 8 : b * 8 + 8, :] = decay
        tall = jnp.concatenate([decay, jnp.zeros((E - 8, E), f32)], axis=0)
        mat = jnp.where(lane == b, tall, mat)
        surv.append(1.0 - jnp.full((1, E), doc[b], jnp.int32).astype(f32))
        start = start * surv[b]
        starts = jnp.where(place == b, start, starts)
        start = start * decay
    dec_ref[32:40, :] = jnp.concatenate(surv + [jnp.zeros((4, E), f32)], axis=0)
    rows = jnp.transpose(mat)
    f = None
    for b in range(4):
        f = surv[b] if b == 0 else f * surv[b]
        f = f * rows[b : b + 1, :]
    sf_ref[...] = starts
    high = f.astype(bf16).astype(f32)
    mid = (f - high).astype(bf16).astype(f32)
    low = f - high - mid
    tile = jnp.concatenate([high, mid, low, jnp.zeros((13, E), f32)], axis=0)
    fx_ref[:, E:] = jnp.zeros((16, HALF - E), bf16)
    fx_ref[:, :E] = tile.astype(bf16)


def prep(doc, ld):
    return pl.pallas_call(
        prep_kernel,
        in_specs=[pl.BlockSpec(memory_space=pltpu.SMEM), VM],
        out_specs=[VM] * 3,
        out_shape=[
            pltpu.VMEM((16, HALF), bf16),
            jax.ShapeDtypeStruct((40, E), f32),
            jax.ShapeDtypeStruct((8, E), f32),
        ],
        compiler_params=params(4),
        name="prep",
    )(doc, ld)


def pre_kernel(
    ld_ref, q_hbm, k_hbm, x_hbm, w_hbm, kd_hbm, x_ref, q_ref, k_ref, w_ref, kd_ref, sems, xsems
):
    half = SPAN // 2
    low = lax.broadcasted_iota(jnp.int32, (half, half), 0) >= lax.broadcasted_iota(
        jnp.int32, (half, half), 1
    )

    def loads(h):
        lanes = pl.ds(pl.multiple_of(h * E, E), E)
        return (
            pltpu.make_async_copy(q_hbm.at[:, lanes], q_ref.at[:, lanes], sems.at[0, h]),
            pltpu.make_async_copy(k_hbm.at[:, lanes], k_ref.at[:, lanes], sems.at[1, h]),
        )

    def stores(h):
        return (
            pltpu.make_async_copy(w_ref.at[h], w_hbm.at[h], sems.at[2, h]),
            pltpu.make_async_copy(kd_ref.at[h], kd_hbm.at[h], sems.at[3, h]),
        )

    for h in range(8):
        for c in loads(h):
            c.start()
    inputs = []
    for r in range(8):
        rows = slice(r * E, (r + 1) * E)
        inputs.append(
            pltpu.make_async_copy(x_hbm.at[rows, :], x_ref.at[rows, :], xsems.at[r])
        )
        inputs[r].start()
    w_ref[:, :, :half, half:] = jnp.zeros((8, 4, half, half), bf16)
    cums = [block_cum(ld_ref[:, b * SPAN : (b + 1) * SPAN]) for b in range(4)]

    def one_head(h, carry):
        for c in loads(h):
            c.wait()
        head = lax.broadcasted_iota(jnp.int32, (8, SPAN), 0) == h
        lanes = pl.ds(pl.multiple_of(h * E, E), E)
        for b in range(4):
            row = jnp.sum(jnp.where(head, cums[b], 0.0), axis=0, keepdims=True)
            col = jnp.transpose(jnp.broadcast_to(row, (8, SPAN)))[:, 0:1]
            last = row[:, SPAN - 1 : SPAN]
            rows = slice(b * SPAN, (b + 1) * SPAN)
            k = k_ref[rows, lanes]
            kt = jnp.transpose(k.astype(f32))
            kd_ref[h, b] = (kt * jnp.exp(last - row)).astype(bf16)
            q = q_ref[rows, lanes]
            s = dot(q[:half], k[:half], ((1,), (1,)))
            g = jnp.exp(jnp.where(low, col[:half] - row[:, :half], -1e30))
            w_ref[h, b, :half, :half] = (s * g).astype(bf16)
            s = dot(q[half:], k, ((1,), (1,)))
            g = jnp.exp(col[half:] - row[:, :half])
            w_ref[h, b, half:, :half] = (s[:, :half] * g).astype(bf16)
            g = jnp.exp(jnp.where(low, col[half:] - row[:, half:], -1e30))
            w_ref[h, b, half:, half:] = (s[:, half:] * g).astype(bf16)
        for c in stores(h):
            c.start()
        return carry

    lax.fori_loop(0, 8, one_head, 0)
    for h in range(8):
        for c in stores(h):
            c.wait()
    for c in inputs:
        c.wait()


def pre(ld, q, k, x):
    shapes = ((8, 4, SPAN, SPAN), (8, 4, E, SPAN))
    return pl.pallas_call(
        pre_kernel,
        in_specs=[VM, HB, HB, HB],
        out_specs=[HB, HB, VM],
        out_shape=[pltpu.HBM(s, bf16) for s in shapes] + [pltpu.VMEM(x.shape, bf16)],
        scratch_shapes=[pltpu.VMEM((1024, 1024), bf16)] * 2
        + [pltpu.VMEM(s, bf16) for s in shapes]
        + [pltpu.SemaphoreType.DMA((4, 8)), pltpu.SemaphoreType.DMA((8,))],
        compiler_params=params(14),
        cost_estimate=pl.CostEstimate(flops=10**9, transcendentals=2 * 10**6, bytes_accessed=10**7),
        name="pre",
    )(ld, hbm(q), hbm(k), hbm(x))


def multiply(mine, d, x_ref, lo, hi, src, dst):
    x, z, core = lax.axis_index("x"), lax.axis_index("z"), lax.axis_index("core")
    first = (core == 0) if mine else (core == 1)
    line = lax.rem(jnp.where(first, x, z) + 4 - d, 4)
    spans = []
    for e in range(4):
        other = lax.rem(jnp.where(first, z, x) + 4 - e, 4)
        at = jnp.where(first, line * LINE + other * CHIP, other * LINE + line * CHIP)
        spans.append(pl.ds(pl.multiple_of(at, 128), CHIP))
    for r in range(2):
        rows = slice(r * 512, (r + 1) * 512)
        part = src[rows, :] if src is not None else None
        for w, (s0, s1) in ((lo, spans[:2]), (hi, spans[2:])):
            lhs = jnp.concatenate([x_ref[rows, s0], x_ref[rows, s1]], axis=1)
            p = dot(lhs, w[: 2 * CHIP, :])
            part = p if part is None else part + p
        dst[rows, :] = part


def mm_kernel(jobs, plane, here, x_ref, *refs):
    n = 2 * len(jobs)
    bufs, refs = refs[:n], refs[n:]
    src = None
    if plane is not None:
        src = refs[0] if plane < 0 else refs[0].at[plane]
        refs = refs[1:]
    out, tails = refs[:2]
    copies = []
    if here:
        wv = bufs
        for j in range(len(jobs)):
            tails[j] = bufs[2 * j][2 * CHIP :, :E]
    else:
        wv, sems = refs[2:]
        for i, b in enumerate(bufs):
            copies.append(
                pltpu.make_async_copy(b.at[: 2 * CHIP, :], wv.at[i], sems.at[i])
            )
        wv = [wv.at[i] for i in range(n)]
        for j in range(len(jobs)):
            copies.append(
                pltpu.make_async_copy(
                    bufs[2 * j].at[2 * CHIP :, :E], tails.at[j], sems.at[n + j]
                )
            )
    for c in copies:
        c.start()
    for j, (mine, d) in enumerate(jobs):
        for c in copies[2 * j : 2 * j + 2]:
            c.wait()
        if plane is None:
            dst, before = out.at[j], None
        else:
            dst, before = out, (out if j else src)
        multiply(mine, d, x_ref, wv[2 * j], wv[2 * j + 1], before, dst)
    for c in copies[n:]:
        c.wait()


def mm(jobs, x, bufs, plane=None, before=None, here=False):
    n = 2 * len(jobs)
    extra = [] if before is None else [before]
    scratch = [] if here else [
        pltpu.VMEM((n, 2 * CHIP, HALF), bf16),
        pltpu.SemaphoreType.DMA((n + len(jobs),)),
    ]
    return pl.pallas_call(
        functools.partial(mm_kernel, jobs, plane, here),
        in_specs=[VM] + [VM if here else HB] * n + [VM] * len(extra),
        out_specs=[VM] * 2,
        out_shape=[
            pltpu.VMEM((ROOM_P, 1024, HALF) if plane is None else (1024, HALF), f32),
            pltpu.VMEM((len(jobs), 64, E), bf16),
        ],
        scratch_shapes=scratch,
        compiler_params=params(6 if here else 10),
        cost_estimate=pl.CostEstimate(
            flops=1024 * LINE * HALF * n, transcendentals=0, bytes_accessed=n * 5 * 10**6
        ),
        name="project",
    )(x, *[(vmem if here else hbm)(a) for a in bufs], *extra)


def head_col(ld_block):
    return jnp.transpose(jnp.exp(block_cum(ld_block)))


def post_kernel(job, dec, q_hbm, kd_hbm, w_hbm, mine_ref, their_ref, x_ref, lo, hi, *refs):
    v_ref, keep_ref, give_ref, tail_ref, st_ref, q_ref, w_ref, acc, kd_ref, sems = refs
    tail_ref[0] = lo[2 * CHIP :, :E]
    core = lax.axis_index("core")
    loads = [
        pltpu.make_async_copy(s, t, sems.at[i])
        for i, (s, t) in enumerate(((kd_hbm, kd_ref), (q_hbm, q_ref), (w_hbm, w_ref)))
    ]
    for c in loads:
        c.start()
    multiply(*job, x_ref, lo, hi, their_ref, acc)
    loads[0].wait()
    states = [None] * 8
    for b in range(4):
        rows = slice(b * SPAN, (b + 1) * SPAN)
        for h in range(8):
            lanes = slice(h * E, (h + 1) * E)
            part = slice((h % 4) * E, (h % 4 + 1) * E)
            v = jnp.where(core == h // 4, mine_ref[rows, part], acc[rows, part]).astype(bf16)
            v_ref[rows, lanes] = v
            state = states[h]
            if b > 0:
                state = state * dec[32 + b : 33 + b, :]
                high = state.astype(bf16)
                st_ref[h, b - 1, :, :E] = high
                st_ref[h, b - 1, :, E:] = (state - high.astype(f32)).astype(bf16)
            update = dot(kd_ref[h, b], v)
            at = b * 8 + h
            states[h] = update if b == 0 else dec[at : at + 1, :] * state + update
    for h in range(4):
        part = slice(h * E, (h + 1) * E)
        keep_ref[part, :] = jnp.where(core == 0, states[h], states[h + 4])
        give_ref[part, :] = jnp.where(core == 0, states[h + 4], states[h])
    for c in loads[1:]:
        c.wait()


def post(job, dec, q, kd, w, mine, theirs, x, bufs):
    return pl.pallas_call(
        functools.partial(post_kernel, job),
        in_specs=[VM, HB, HB, HB] + [VM] * (3 + len(bufs)),
        out_specs=[VM] * 7,
        out_shape=[
            pltpu.VMEM((1024, 1024), bf16),
            pltpu.VMEM((HALF, E), f32),
            pltpu.VMEM((HALF, E), f32),
            pltpu.VMEM((1, 64, E), bf16),
            pltpu.VMEM((8, 3, E, 2 * E), bf16),
            pltpu.VMEM((1024, 1024), bf16),
            pltpu.VMEM((8, 4, SPAN, SPAN), bf16),
        ],
        scratch_shapes=[
            pltpu.VMEM((1024, HALF), f32),
            pltpu.VMEM((8, 4, E, SPAN), bf16),
            pltpu.SemaphoreType.DMA((3,)),
        ],
        compiler_params=params(10),
        name="post",
    )(dec, hbm(q), hbm(kd), hbm(w), mine, theirs, x, *bufs)


def within_kernel(ld_ref, v_ref, st_ref, q_ref, w_ref, comb_ref):
    half = SPAN // 2
    for b in range(4):
        rows = slice(b * SPAN, (b + 1) * SPAN)
        col = head_col(ld_ref[:, rows])
        for h in range(8):
            lanes = slice(h * E, (h + 1) * E)
            v = v_ref[rows, lanes]
            top = dot(w_ref[h, b, :half, :half], v[:half])
            low = dot(w_ref[h, b, half:, :], v)
            inner = jnp.concatenate([top, low], axis=0)
            if b > 0:
                o = dot(q_ref[rows, lanes], st_ref[h, b - 1])
                inner = inner + col[:, h : h + 1] * (o[:, :E] + o[:, E:])
            comb_ref[0, rows, lanes] = inner


def within(ld, v, st, q, w):
    return pl.pallas_call(
        within_kernel,
        in_specs=[VM] * 5,
        out_specs=VM,
        out_shape=pltpu.VMEM((ROOM, 1024, 1024), f32),
        compiler_params=params(6),
        cost_estimate=pl.CostEstimate(
            flops=3 * 10**9, transcendentals=0, bytes_accessed=10**7
        ),
        name="within",
    )(ld, v, st, q, w)


def weights_kernel(t_own, t_mine, t_op, t_up, t_last, t_dn, out_ref):
    x, z, core = lax.axis_index("x"), lax.axis_index("z"), lax.axis_index("core")
    first = core == 0

    def factors(tiles):
        out = []
        for t in tiles:
            t = t.astype(f32)
            for e in range(4):
                r = [t[16 * e + i : 16 * e + i + 1] for i in range(3)]
                out.append(r[0] + r[1] + r[2])
        return out

    near = factors((t_own[0], t_mine[0], t_op[0], t_mine[1]))
    far = factors((t_own[1], t_up[0], t_last[0], t_dn[0]))
    own = [near[0], far[0]]
    rows = [near[4 * n + e] * far[4 * e + n] for n in range(4) for e in range(4)]
    g = jnp.concatenate(rows, axis=0)
    n = lax.broadcasted_iota(jnp.int32, (16, E), 0)
    px = jnp.where(first, n // 4, n % 4)
    pz = jnp.where(first, n % 4, n // 4)
    k_at = ((x + 4 - px) % 4) * 4 + (z + 4 - pz) % 4
    out = []
    for d in range(4):
        tgt = jnp.where(first, lax.rem(x + d, 4) * 4 + z, x * 4 + lax.rem(z + d, 4))
        for e in range(4):
            src = jnp.where(
                first, x * 4 + lax.rem(z + 4 - e, 4), lax.rem(x + 4 - e, 4) * 4 + z
            )
            p = jnp.where((k_at > src) & (k_at < tgt), g, 1.0)
            p = p[:8] * p[8:]
            p = p[:4] * p[4:]
            p = p[:2] * p[2:]
            p = p[:1] * p[1:]
            out.append(jnp.where(src < tgt, p, 0.0))
    flat = jnp.concatenate(out + own + [jnp.zeros((E - 18, E), f32)], axis=0)
    turned = jnp.transpose(flat)
    out_ref[...] = jnp.where(first, turned[:8], jnp.concatenate([turned[4:8]] * 2, axis=0))


def weights(*tails):
    return pl.pallas_call(
        weights_kernel,
        in_specs=[VM] * 6,
        out_specs=VM,
        out_shape=pltpu.VMEM((8, E), f32),
        compiler_params=params(4),
        name="weights",
    )(*tails)


def one(ref, h, i):
    return jnp.broadcast_to(ref[h : h + 1, i : i + 1], (E, E))


def chip_kernel(wt, own_ref, recv_ref, f_ref, b_ref):
    first = lax.axis_index("core") == 0
    for h in range(4):
        r = slice(h * E, (h + 1) * E)
        a, b = own_ref[r, :], recv_ref[r, :]
        s = jnp.where(first, one(wt, h, 17) * a + b, a + one(wt, h, 16) * b)
        f_ref[r, :] = s
        b_ref[r, :] = s.astype(bf16)


def spread_kernel(wt, own_ref, r1, r2, r3, o0, o1, o2, o3):
    for h in range(4):
        r = slice(h * E, (h + 1) * E)
        src = [own_ref[r, :]] + [a[r, :].astype(f32) for a in (r1, r2, r3)]
        for d, o in enumerate((o0, o1, o2, o3)):
            s = None
            for e in range(4):
                t = one(wt, h, d * 4 + e) * src[e]
                s = t if s is None else s + t
            o[r, :] = s.astype(o.dtype)


def enter_kernel(wt, m0, r1, r2, r3, own_ref, recv_ref, mine_ref, other_ref):
    first = lax.axis_index("core") == 0
    for h in range(4):
        r = slice(h * E, (h + 1) * E)
        i = m0[r, :]
        for a in (r1, r2, r3):
            i = i + a[r, :].astype(f32)
        mine_ref[r, :] = jnp.where(first, i, one(wt, h, 17) * i + recv_ref[r, :])
        other_ref[r, :] = jnp.where(first, one(wt, h, 16) * i + own_ref[r, :], i)


def small(kernel, name, args, outs):
    return pl.pallas_call(
        kernel,
        in_specs=[VM] * len(args),
        out_specs=[VM] * len(outs),
        out_shape=[pltpu.VMEM((HALF, E), t) for t in outs],
        compiler_params=params(4),
        name=name,
    )(*args)


def outer_kernel(side, sf, ld_ref, state_ref, comb_ref, q_ref, *refs):
    before, (out_ref, sq_ref) = refs[:-2], refs[-2:]
    core = lax.axis_index("core")
    half = core if side == 0 else 1 - core
    pairs = []
    for h in range(4):
        m = state_ref[h * E : (h + 1) * E, :]
        high = m.astype(bf16)
        pairs.append(jnp.concatenate([high, (m - high.astype(f32)).astype(bf16)], axis=1))
    for b in range(4):
        rows = slice(b * SPAN, (b + 1) * SPAN)
        scale = jnp.exp(block_cum(ld_ref[:, rows])) * sf[:, b : b + 1]
        scale = jnp.where(half == 0, scale[:4], scale[4:])
        col = jnp.transpose(jnp.concatenate([scale, scale], axis=0))
        total = None
        for h in range(4):
            lanes = pl.ds(pl.multiple_of(half * HALF + h * E, E), E)
            o = dot(q_ref[rows, lanes], pairs[h])
            o = (o[:, :E] + o[:, E:]) * col[:, h : h + 1]
            o = comb_ref[0, rows, lanes] + o
            out_ref[rows, h * E : (h + 1) * E] = o
            total = o * o if total is None else total + o * o
        for t in range(2):
            tt = jnp.transpose(total[t * E : (t + 1) * E, :])
            r = slice(b * 2 + t, b * 2 + t + 1)
            sq = jnp.sum(tt, axis=0, keepdims=True)
            sq_ref[r, :] = sq + before[0][r, :] if before else sq


def outer(side, sf, ld, state, comb, q, *before):
    return pl.pallas_call(
        functools.partial(outer_kernel, side),
        in_specs=[VM] * (5 + len(before)),
        out_specs=[VM, VM],
        out_shape=[pltpu.VMEM((1024, HALF), f32), pltpu.VMEM((8, E), f32)],
        compiler_params=params(6),
        cost_estimate=pl.CostEstimate(
            flops=6 * 10**8, transcendentals=0, bytes_accessed=6 * 10**6
        ),
        name="outer",
    )(sf, ld, state, comb, q, *before)


def norm_kernel(mine_ref, other_ref, s0, s1, s2, s3, gain_ref, y_hbm, y_ref, sems):
    core = lax.axis_index("core")
    total = s0[...] + s1[...] + s2[...] + s3[...]
    scale = lax.rsqrt(total / (SHARD_ATTN_PARTS * E) + 1e-06)
    copies = []
    for t in range(8):
        col = jnp.transpose(jnp.broadcast_to(scale[t : t + 1, :], (E, E)))
        rows = slice(t * E, (t + 1) * E)
        for ref, half in ((mine_ref, core), (other_ref, 1 - core)):
            for h in range(4):
                lanes = pl.ds(pl.multiple_of(half * HALF + h * E, E), E)
                y = ref[rows, h * E : (h + 1) * E] * col * gain_ref[:, lanes]
                y_ref[rows, lanes] = y.astype(bf16)
        c = pltpu.make_async_copy(y_ref.at[rows, :], y_hbm.at[rows, :], sems.at[t])
        c.start()
        copies.append(c)
    for c in copies:
        c.wait()


def norm(mine, other, sqs, gain):
    return pl.pallas_call(
        norm_kernel,
        in_specs=[VM] * 7,
        out_specs=HB,
        out_shape=jax.ShapeDtypeStruct((1024, 1024), bf16),
        scratch_shapes=[pltpu.VMEM((1024, 1024), bf16), pltpu.SemaphoreType.DMA((8,))],
        compiler_params=params(8),
        name="norm",
    )(mine, other, *sqs, gain)


def per_device(inputs, q, k, value_weight, ld, doc_start, gain):
    x, z, core = lax.axis_index("x"), lax.axis_index("z"), lax.axis_index("core")
    first = core == 0
    bar = lax.optimization_barrier

    my_w = lax.dynamic_slice(value_weight, (0, core * HALF), (CHIP // 2, HALF))
    their_w = lax.dynamic_slice(value_weight, (0, (1 - core) * HALF), (CHIP // 2, HALF))
    recv_w = swap(their_w)
    fx, dec, sf = prep(doc_start, ld)
    chip_w = jnp.where(
        first,
        jnp.concatenate([my_w, recv_w, fx], axis=0),
        jnp.concatenate([recv_w, my_w, fx], axis=0),
    )
    rows = CHIP // 2
    up = crossed(chip_w, "z", "x", 1, 1)
    dn = crossed(chip_w, "z", "x", -1, -1)
    far_a = crossed(up[:rows], "z", "x", 1, 1)
    far_b = crossed(dn[rows:], "z", "x", -1, -1)
    chip_w, up, dn, far_a, far_b, ld, q, k = bar((chip_w, up, dn, far_a, far_b, ld, q, k))
    p_lo = jnp.concatenate(
        [chip_w[:CHIP], up[:CHIP], chip_w[CHIP:], up[CHIP:], far_b[rows:], dn[CHIP:]], axis=0
    )
    p_hi = jnp.concatenate([far_a, far_b[:rows], dn[:CHIP]], axis=0)
    up_lo = crossed(p_lo, "x", "z", 1, 1)
    dn_hi = crossed(p_hi, "x", "z", -1, -1)
    up_hi = crossed(p_hi, "x", "z", 1, 1)
    dn_lo = crossed(p_lo, "x", "z", -1, -1)
    s_lo, s_hi = swap(p_lo), swap(p_hi)
    s_lo, s_hi, ld, q, k = bar((s_lo, s_hi, ld, q, k))
    w, kd, xv = pre(ld, q, k, inputs)
    bufs = (p_lo, p_hi, s_lo, s_hi)
    sums, t_own = mm(((True, 0), (False, 0)), xv, bufs, here=True)
    up_lo, dn_hi, sums = bar((up_lo, dn_hi, sums))
    op_lo = crossed(up_lo, "x", "z", 1, 1)
    op_hi = crossed(dn_hi, "x", "z", -1, -1)
    up_lo, up_hi, dn_lo, dn_hi = bar((up_lo, up_hi, dn_lo, dn_hi))
    swapped = (swap(up_lo), swap(up_hi))
    bufs = (up_lo, up_hi, dn_lo, dn_hi)
    mine, t_mine = mm(((True, 1), (True, 3)), xv, bufs, 0, sums, True)
    op_lo, op_hi, dn_lo, dn_hi, mine = bar((op_lo, op_hi, dn_lo, dn_hi, mine))
    theirs, t_up = mm(((False, 1),), xv, swapped, 1, sums, True)
    theirs, t_dn = mm(((False, 3),), xv, (swap(dn_lo), swap(dn_hi)), -1, theirs, True)
    mine, t_op = mm(((True, 2),), xv, (op_lo, op_hi), -1, mine, True)
    bufs = [swap(op_lo), swap(op_hi)]
    v, own, give, t_last, st, qv, wv = post(
        (False, 2), vmem(dec), q, kd, w, mine, theirs, xv, [vmem(a) for a in bufs]
    )
    recv = vmem(swap(give))
    wt = weights(t_own, t_mine, t_op, t_up, t_last, t_dn)
    chip, chip16 = small(chip_kernel, "chip", (wt, own, recv), (f32, bf16))
    got = [vmem(crossed(chip16, "z", "x", d, d)) for d in (1, 2, 3)]
    v, chip = bar((v, chip))
    comb = within(ld, v, st, qv, wv)
    *got, comb = bar((*got, comb))
    sent = small(spread_kernel, "spread", (wt, chip, *got), (f32, bf16, bf16, bf16))
    got = [vmem(crossed(sent[d], "x", "z", d, d)) for d in (1, 2, 3)]
    state, give = small(enter_kernel, "enter", (wt, sent[0], *got, own, recv), (f32, f32))
    sf, qv = vmem(sf), vmem(q)
    mine, sq = outer(0, sf, ld, state, comb, qv)
    other, sq = outer(1, sf, ld, vmem(swap(give)), comb, qv, sq)
    sqs = [sq] + [vmem(ring(sq, "head", d)) for d in (1, 2, 3)]
    return norm(mine, other, sqs, gain.reshape(1, -1))


def solution(mesh):
    mesh = Mesh(mesh.devices.reshape(4, 4, 2, 4), ("x", "z", "core", "head"))
    placed = (
        P(SEQ, None),
        P(SEQ, "head"),
        P(SEQ, "head"),
        P(SEQ, "head"),
        P("head", SEQ),
        P(SEQ),
        P("head"),
    )
    return jax.shard_map(
        per_device, mesh=mesh, in_specs=placed, out_specs=P(SEQ, "head"), check_vma=False
    )
```

```python
import functools
import jax
import jax.numpy as jnp
from jax import lax
from jax.experimental import pallas as pl
from jax.experimental.pallas import tpu as pltpu
from jax.sharding import Mesh, PartitionSpec as P

SHARD_ATTN_PARTS = 32
E = 128
SPAN = 256
SEQ = ("x", "z", "core")
SWAP = [(0, 1), (1, 0)]
VM = pl.BlockSpec(memory_space=pltpu.VMEM)
HB = pl.BlockSpec(memory_space=pltpu.HBM)
MIB = 1024 * 1024
HALF = 512
LINE = 1536
CHIP = 384
ROOM = 2
ROOM_P = 4
f32, bf16 = jnp.float32, jnp.bfloat16


def swap(a):
    return lax.ppermute(a, "core", SWAP)


def ring(a, axis, step):
    return lax.ppermute(a, axis, [(i, (i + step) % 4) for i in range(4)])


def crossed(a, first, second, step0, step1):
    pairs = []
    for x in range(4):
        for z in range(4):
            for c in range(2):
                axis, step = ((first, step0), (second, step1))[c]
                tx = (x + step) % 4 if axis == "x" else x
                tz = (z + step) % 4 if axis == "z" else z
                pairs.append((x * 8 + z * 2 + c, tx * 8 + tz * 2 + c))
    return lax.ppermute(a, SEQ, pairs)


def dot(a, b, dims=((1,), (0,))):
    return lax.dot_general(a, b, (dims, ((), ())), preferred_element_type=f32)


def block_cum(ld):
    lane = lax.broadcasted_iota(jnp.int32, ld.shape, 1)
    step = 1
    while step < SPAN:
        ld = ld + jnp.where(lane >= step, pltpu.roll(ld, step, 1), 0.0)
        step *= 2
    return ld


def vmem(a):
    return pltpu.with_memory_space_constraint(a, pltpu.VMEM)


def hbm(a):
    return pltpu.with_memory_space_constraint(a, pltpu.HBM)


def params(mib):
    return pltpu.CompilerParams(vmem_limit_bytes=mib * MIB)


def prep_kernel(doc, ld_ref, fx_ref, dec_ref, sf_ref):
    lane = lax.broadcasted_iota(jnp.int32, (E, E), 1)
    mat = jnp.zeros((E, E), f32)
    place = lax.broadcasted_iota(jnp.int32, (8, E), 1)
    start = jnp.ones((8, E), f32)
    starts = jnp.zeros((8, E), f32)
    surv = []
    for b in range(4):
        total = jnp.sum(ld_ref[:, b * SPAN : (b + 1) * SPAN], axis=1, keepdims=True)
        decay = jnp.broadcast_to(jnp.exp(total), (8, E))
        dec_ref[b * 8 : b * 8 + 8, :] = decay
        tall = jnp.concatenate([decay, jnp.zeros((E - 8, E), f32)], axis=0)
        mat = jnp.where(lane == b, tall, mat)
        surv.append(1.0 - jnp.full((1, E), doc[b], jnp.int32).astype(f32))
        start = start * surv[b]
        starts = jnp.where(place == b, start, starts)
        start = start * decay
    dec_ref[32:40, :] = jnp.concatenate(surv + [jnp.zeros((4, E), f32)], axis=0)
    rows = jnp.transpose(mat)
    f = None
    for b in range(4):
        f = surv[b] if b == 0 else f * surv[b]
        f = f * rows[b : b + 1, :]
    sf_ref[...] = starts
    high = f.astype(bf16).astype(f32)
    mid = (f - high).astype(bf16).astype(f32)
    low = f - high - mid
    tile = jnp.concatenate([high, mid, low, jnp.zeros((13, E), f32)], axis=0)
    fx_ref[:, E:] = jnp.zeros((16, HALF - E), bf16)
    fx_ref[:, :E] = tile.astype(bf16)


def prep(doc, ld):
    return pl.pallas_call(
        prep_kernel,
        in_specs=[pl.BlockSpec(memory_space=pltpu.SMEM), VM],
        out_specs=[VM] * 3,
        out_shape=[
            pltpu.VMEM((16, HALF), bf16),
            jax.ShapeDtypeStruct((40, E), f32),
            jax.ShapeDtypeStruct((8, E), f32),
        ],
        compiler_params=params(4),
        name="prep",
    )(doc, ld)


def pre_kernel(
    ld_ref, q_hbm, k_hbm, x_hbm, w_hbm, kd_hbm, x_ref, q_ref, k_ref, w_ref, kd_ref, sems, xsems
):
    half = SPAN // 2
    low = lax.broadcasted_iota(jnp.int32, (half, half), 0) >= lax.broadcasted_iota(
        jnp.int32, (half, half), 1
    )

    def loads(h):
        lanes = pl.ds(pl.multiple_of(h * E, E), E)
        return (
            pltpu.make_async_copy(q_hbm.at[:, lanes], q_ref.at[:, lanes], sems.at[0, h]),
            pltpu.make_async_copy(k_hbm.at[:, lanes], k_ref.at[:, lanes], sems.at[1, h]),
        )

    def stores(h):
        return (
            pltpu.make_async_copy(w_ref.at[h], w_hbm.at[h], sems.at[2, h]),
            pltpu.make_async_copy(kd_ref.at[h], kd_hbm.at[h], sems.at[3, h]),
        )

    for h in range(8):
        for c in loads(h):
            c.start()
    inputs = []
    for r in range(8):
        rows = slice(r * E, (r + 1) * E)
        inputs.append(
            pltpu.make_async_copy(x_hbm.at[rows, :], x_ref.at[rows, :], xsems.at[r])
        )
        inputs[r].start()
    w_ref[:, :, :half, half:] = jnp.zeros((8, 4, half, half), bf16)
    cums = [block_cum(ld_ref[:, b * SPAN : (b + 1) * SPAN]) for b in range(4)]

    def one_head(h, carry):
        for c in loads(h):
            c.wait()
        head = lax.broadcasted_iota(jnp.int32, (8, SPAN), 0) == h
        lanes = pl.ds(pl.multiple_of(h * E, E), E)
        for b in range(4):
            row = jnp.sum(jnp.where(head, cums[b], 0.0), axis=0, keepdims=True)
            col = jnp.transpose(jnp.broadcast_to(row, (8, SPAN)))[:, 0:1]
            last = row[:, SPAN - 1 : SPAN]
            rows = slice(b * SPAN, (b + 1) * SPAN)
            k = k_ref[rows, lanes]
            kt = jnp.transpose(k.astype(f32))
            kd_ref[h, b] = (kt * jnp.exp(last - row)).astype(bf16)
            q = q_ref[rows, lanes]
            s = dot(q[:half], k[:half], ((1,), (1,)))
            g = jnp.exp(jnp.where(low, col[:half] - row[:, :half], -1e30))
            w_ref[h, b, :half, :half] = (s * g).astype(bf16)
            s = dot(q[half:], k, ((1,), (1,)))
            g = jnp.exp(col[half:] - row[:, :half])
            w_ref[h, b, half:, :half] = (s[:, :half] * g).astype(bf16)
            g = jnp.exp(jnp.where(low, col[half:] - row[:, half:], -1e30))
            w_ref[h, b, half:, half:] = (s[:, half:] * g).astype(bf16)
        for c in stores(h):
            c.start()
        return carry

    lax.fori_loop(0, 8, one_head, 0)
    for h in range(8):
        for c in stores(h):
            c.wait()
    for c in inputs:
        c.wait()


def pre(ld, q, k, x):
    shapes = ((8, 4, SPAN, SPAN), (8, 4, E, SPAN))
    return pl.pallas_call(
        pre_kernel,
        in_specs=[VM, HB, HB, HB],
        out_specs=[HB, HB, VM],
        out_shape=[pltpu.HBM(s, bf16) for s in shapes] + [pltpu.VMEM(x.shape, bf16)],
        scratch_shapes=[pltpu.VMEM((1024, 1024), bf16)] * 2
        + [pltpu.VMEM(s, bf16) for s in shapes]
        + [pltpu.SemaphoreType.DMA((4, 8)), pltpu.SemaphoreType.DMA((8,))],
        compiler_params=params(14),
        cost_estimate=pl.CostEstimate(flops=10**9, transcendentals=2 * 10**6, bytes_accessed=10**7),
        name="pre",
    )(ld, hbm(q), hbm(k), hbm(x))


def multiply(mine, d, x_ref, lo, hi, src, dst):
    x, z, core = lax.axis_index("x"), lax.axis_index("z"), lax.axis_index("core")
    first = (core == 0) if mine else (core == 1)
    line = lax.rem(jnp.where(first, x, z) + 4 - d, 4)
    spans = []
    for e in range(4):
        other = lax.rem(jnp.where(first, z, x) + 4 - e, 4)
        at = jnp.where(first, line * LINE + other * CHIP, other * LINE + line * CHIP)
        spans.append(pl.ds(pl.multiple_of(at, 128), CHIP))
    for r in range(2):
        rows = slice(r * 512, (r + 1) * 512)
        part = src[rows, :] if src is not None else None
        for w, (s0, s1) in ((lo, spans[:2]), (hi, spans[2:])):
            lhs = jnp.concatenate([x_ref[rows, s0], x_ref[rows, s1]], axis=1)
            p = dot(lhs, w[: 2 * CHIP, :])
            part = p if part is None else part + p
        dst[rows, :] = part


def mm_kernel(jobs, plane, here, x_ref, *refs):
    n = 2 * len(jobs)
    bufs, refs = refs[:n], refs[n:]
    src = None
    if plane is not None:
        src = refs[0] if plane < 0 else refs[0].at[plane]
        refs = refs[1:]
    out, tails = refs[:2]
    copies = []
    if here:
        wv = bufs
        for j in range(len(jobs)):
            tails[j] = bufs[2 * j][2 * CHIP :, :E]
    else:
        wv, sems = refs[2:]
        for i, b in enumerate(bufs):
            copies.append(
                pltpu.make_async_copy(b.at[: 2 * CHIP, :], wv.at[i], sems.at[i])
            )
        wv = [wv.at[i] for i in range(n)]
        for j in range(len(jobs)):
            copies.append(
                pltpu.make_async_copy(
                    bufs[2 * j].at[2 * CHIP :, :E], tails.at[j], sems.at[n + j]
                )
            )
    for c in copies:
        c.start()
    for j, (mine, d) in enumerate(jobs):
        for c in copies[2 * j : 2 * j + 2]:
            c.wait()
        if plane is None:
            dst, before = out.at[j], None
        else:
            dst, before = out, (out if j else src)
        multiply(mine, d, x_ref, wv[2 * j], wv[2 * j + 1], before, dst)
    for c in copies[n:]:
        c.wait()


def mm(jobs, x, bufs, plane=None, before=None, here=False):
    n = 2 * len(jobs)
    extra = [] if before is None else [before]
    scratch = [] if here else [
        pltpu.VMEM((n, 2 * CHIP, HALF), bf16),
        pltpu.SemaphoreType.DMA((n + len(jobs),)),
    ]
    return pl.pallas_call(
        functools.partial(mm_kernel, jobs, plane, here),
        in_specs=[VM] + [VM if here else HB] * n + [VM] * len(extra),
        out_specs=[VM] * 2,
        out_shape=[
            pltpu.VMEM((ROOM_P, 1024, HALF) if plane is None else (1024, HALF), f32),
            pltpu.VMEM((len(jobs), 64, E), bf16),
        ],
        scratch_shapes=scratch,
        compiler_params=params(6 if here else 10),
        cost_estimate=pl.CostEstimate(
            flops=1024 * LINE * HALF * n, transcendentals=0, bytes_accessed=n * 5 * 10**6
        ),
        name="project",
    )(x, *[(vmem if here else hbm)(a) for a in bufs], *extra)


def head_col(ld_block):
    return jnp.transpose(jnp.exp(block_cum(ld_block)))


def post_kernel(job, dec, q_hbm, kd_hbm, w_hbm, mine_ref, their_ref, x_ref, lo, hi, *refs):
    v_ref, keep_ref, give_ref, tail_ref, st_ref, q_ref, w_ref, acc, kd_ref, sems = refs
    tail_ref[0] = lo[2 * CHIP :, :E]
    core = lax.axis_index("core")
    loads = [
        pltpu.make_async_copy(s, t, sems.at[i])
        for i, (s, t) in enumerate(((kd_hbm, kd_ref), (q_hbm, q_ref), (w_hbm, w_ref)))
    ]
    for c in loads:
        c.start()
    multiply(*job, x_ref, lo, hi, their_ref, acc)
    loads[0].wait()
    states = [None] * 8
    for b in range(4):
        rows = slice(b * SPAN, (b + 1) * SPAN)
        for h in range(8):
            lanes = slice(h * E, (h + 1) * E)
            part = slice((h % 4) * E, (h % 4 + 1) * E)
            v = jnp.where(core == h // 4, mine_ref[rows, part], acc[rows, part]).astype(bf16)
            v_ref[rows, lanes] = v
            state = states[h]
            if b > 0:
                state = state * dec[32 + b : 33 + b, :]
                high = state.astype(bf16)
                st_ref[h, b - 1, :, :E] = high
                st_ref[h, b - 1, :, E:] = (state - high.astype(f32)).astype(bf16)
            update = dot(kd_ref[h, b], v)
            at = b * 8 + h
            states[h] = update if b == 0 else dec[at : at + 1, :] * state + update
    for h in range(4):
        part = slice(h * E, (h + 1) * E)
        keep_ref[part, :] = jnp.where(core == 0, states[h], states[h + 4])
        give_ref[part, :] = jnp.where(core == 0, states[h + 4], states[h])
    for c in loads[1:]:
        c.wait()


def post(job, dec, q, kd, w, mine, theirs, x, bufs):
    return pl.pallas_call(
        functools.partial(post_kernel, job),
        in_specs=[VM, HB, HB, HB] + [VM] * (3 + len(bufs)),
        out_specs=[VM] * 7,
        out_shape=[
            pltpu.VMEM((1024, 1024), bf16),
            pltpu.VMEM((HALF, E), f32),
            pltpu.VMEM((HALF, E), f32),
            pltpu.VMEM((1, 64, E), bf16),
            pltpu.VMEM((8, 3, E, 2 * E), bf16),
            pltpu.VMEM((1024, 1024), bf16),
            pltpu.VMEM((8, 4, SPAN, SPAN), bf16),
        ],
        scratch_shapes=[
            pltpu.VMEM((1024, HALF), f32),
            pltpu.VMEM((8, 4, E, SPAN), bf16),
            pltpu.SemaphoreType.DMA((3,)),
        ],
        compiler_params=params(10),
        name="post",
    )(dec, hbm(q), hbm(kd), hbm(w), mine, theirs, x, *bufs)


def within_kernel(ld_ref, v_ref, st_ref, q_ref, w_ref, comb_ref):
    half = SPAN // 2
    for b in range(4):
        rows = slice(b * SPAN, (b + 1) * SPAN)
        col = head_col(ld_ref[:, rows])
        for h in range(8):
            lanes = slice(h * E, (h + 1) * E)
            v = v_ref[rows, lanes]
            top = dot(w_ref[h, b, :half, :half], v[:half])
            low = dot(w_ref[h, b, half:, :], v)
            inner = jnp.concatenate([top, low], axis=0)
            if b > 0:
                o = dot(q_ref[rows, lanes], st_ref[h, b - 1])
                inner = inner + col[:, h : h + 1] * (o[:, :E] + o[:, E:])
            comb_ref[0, rows, lanes] = inner


def within(ld, v, st, q, w):
    return pl.pallas_call(
        within_kernel,
        in_specs=[VM] * 5,
        out_specs=VM,
        out_shape=pltpu.VMEM((ROOM, 1024, 1024), f32),
        compiler_params=params(6),
        cost_estimate=pl.CostEstimate(
            flops=3 * 10**9, transcendentals=0, bytes_accessed=10**7
        ),
        name="within",
    )(ld, v, st, q, w)


def weights_kernel(t_own, t_mine, t_op, t_up, t_last, t_dn, out_ref):
    x, z, core = lax.axis_index("x"), lax.axis_index("z"), lax.axis_index("core")
    first = core == 0

    def factors(tiles):
        out = []
        for t in tiles:
            t = t.astype(f32)
            for e in range(4):
                r = [t[16 * e + i : 16 * e + i + 1] for i in range(3)]
                out.append(r[0] + r[1] + r[2])
        return out

    near = factors((t_own[0], t_mine[0], t_op[0], t_mine[1]))
    far = factors((t_own[1], t_up[0], t_last[0], t_dn[0]))
    own = [near[0], far[0]]
    rows = [near[4 * n + e] * far[4 * e + n] for n in range(4) for e in range(4)]
    g = jnp.concatenate(rows, axis=0)
    n = lax.broadcasted_iota(jnp.int32, (16, E), 0)
    px = jnp.where(first, n // 4, n % 4)
    pz = jnp.where(first, n % 4, n // 4)
    k_at = ((x + 4 - px) % 4) * 4 + (z + 4 - pz) % 4
    out = []
    for d in range(4):
        tgt = jnp.where(first, lax.rem(x + d, 4) * 4 + z, x * 4 + lax.rem(z + d, 4))
        for e in range(4):
            src = jnp.where(
                first, x * 4 + lax.rem(z + 4 - e, 4), lax.rem(x + 4 - e, 4) * 4 + z
            )
            p = jnp.where((k_at > src) & (k_at < tgt), g, 1.0)
            p = p[:8] * p[8:]
            p = p[:4] * p[4:]
            p = p[:2] * p[2:]
            p = p[:1] * p[1:]
            out.append(jnp.where(src < tgt, p, 0.0))
    flat = jnp.concatenate(out + own + [jnp.zeros((E - 18, E), f32)], axis=0)
    turned = jnp.transpose(flat)
    out_ref[...] = jnp.where(first, turned[:8], jnp.concatenate([turned[4:8]] * 2, axis=0))


def weights(*tails):
    return pl.pallas_call(
        weights_kernel,
        in_specs=[VM] * 6,
        out_specs=VM,
        out_shape=pltpu.VMEM((8, E), f32),
        compiler_params=params(4),
        name="weights",
    )(*tails)


def one(ref, h, i):
    return jnp.broadcast_to(ref[h : h + 1, i : i + 1], (E, E))


def chip_kernel(wt, own_ref, recv_ref, f_ref, b_ref):
    first = lax.axis_index("core") == 0
    for h in range(4):
        r = slice(h * E, (h + 1) * E)
        a, b = own_ref[r, :], recv_ref[r, :]
        s = jnp.where(first, one(wt, h, 17) * a + b, a + one(wt, h, 16) * b)
        f_ref[r, :] = s
        b_ref[r, :] = s.astype(bf16)


def spread_kernel(wt, own_ref, r1, r2, r3, o0, o1, o2, o3):
    for h in range(4):
        r = slice(h * E, (h + 1) * E)
        src = [own_ref[r, :]] + [a[r, :].astype(f32) for a in (r1, r2, r3)]
        for d, o in enumerate((o0, o1, o2, o3)):
            s = None
            for e in range(4):
                t = one(wt, h, d * 4 + e) * src[e]
                s = t if s is None else s + t
            o[r, :] = s.astype(o.dtype)


def enter_kernel(wt, m0, r1, r2, r3, own_ref, recv_ref, mine_ref, other_ref):
    first = lax.axis_index("core") == 0
    for h in range(4):
        r = slice(h * E, (h + 1) * E)
        i = m0[r, :]
        for a in (r1, r2, r3):
            i = i + a[r, :].astype(f32)
        mine_ref[r, :] = jnp.where(first, i, one(wt, h, 17) * i + recv_ref[r, :])
        other_ref[r, :] = jnp.where(first, one(wt, h, 16) * i + own_ref[r, :], i)


def small(kernel, name, args, outs):
    return pl.pallas_call(
        kernel,
        in_specs=[VM] * len(args),
        out_specs=[VM] * len(outs),
        out_shape=[pltpu.VMEM((HALF, E), t) for t in outs],
        compiler_params=params(4),
        name=name,
    )(*args)


def outer_kernel(side, sf, ld_ref, state_ref, comb_ref, q_ref, *refs):
    before, (out_ref, sq_ref) = refs[:-2], refs[-2:]
    core = lax.axis_index("core")
    half = core if side == 0 else 1 - core
    pairs = []
    for h in range(4):
        m = state_ref[h * E : (h + 1) * E, :]
        high = m.astype(bf16)
        pairs.append(jnp.concatenate([high, (m - high.astype(f32)).astype(bf16)], axis=1))
    for b in range(4):
        rows = slice(b * SPAN, (b + 1) * SPAN)
        scale = jnp.exp(block_cum(ld_ref[:, rows])) * sf[:, b : b + 1]
        scale = jnp.where(half == 0, scale[:4], scale[4:])
        col = jnp.transpose(jnp.concatenate([scale, scale], axis=0))
        total = None
        for h in range(4):
            lanes = pl.ds(pl.multiple_of(half * HALF + h * E, E), E)
            o = dot(q_ref[rows, lanes], pairs[h])
            o = (o[:, :E] + o[:, E:]) * col[:, h : h + 1]
            o = comb_ref[0, rows, lanes] + o
            out_ref[rows, h * E : (h + 1) * E] = o
            total = o * o if total is None else total + o * o
        for t in range(2):
            tt = jnp.transpose(total[t * E : (t + 1) * E, :])
            r = slice(b * 2 + t, b * 2 + t + 1)
            sq = jnp.sum(tt, axis=0, keepdims=True)
            sq_ref[r, :] = sq + before[0][r, :] if before else sq


def outer(side, sf, ld, state, comb, q, *before):
    return pl.pallas_call(
        functools.partial(outer_kernel, side),
        in_specs=[VM] * (5 + len(before)),
        out_specs=[VM, VM],
        out_shape=[pltpu.VMEM((1024, HALF), f32), pltpu.VMEM((8, E), f32)],
        compiler_params=params(6),
        cost_estimate=pl.CostEstimate(
            flops=6 * 10**8, transcendentals=0, bytes_accessed=6 * 10**6
        ),
        name="outer",
    )(sf, ld, state, comb, q, *before)


def norm_kernel(mine_ref, other_ref, s0, s1, s2, s3, gain_ref, y_hbm, y_ref, sems):
    core = lax.axis_index("core")
    total = s0[...] + s1[...] + s2[...] + s3[...]
    scale = lax.rsqrt(total / (SHARD_ATTN_PARTS * E) + 1e-06)
    copies = []
    for t in range(8):
        col = jnp.transpose(jnp.broadcast_to(scale[t : t + 1, :], (E, E)))
        rows = slice(t * E, (t + 1) * E)
        for ref, half in ((mine_ref, core), (other_ref, 1 - core)):
            for h in range(4):
                lanes = pl.ds(pl.multiple_of(half * HALF + h * E, E), E)
                y = ref[rows, h * E : (h + 1) * E] * col * gain_ref[:, lanes]
                y_ref[rows, lanes] = y.astype(bf16)
        c = pltpu.make_async_copy(y_ref.at[rows, :], y_hbm.at[rows, :], sems.at[t])
        c.start()
        copies.append(c)
    for c in copies:
        c.wait()


def norm(mine, other, sqs, gain):
    return pl.pallas_call(
        norm_kernel,
        in_specs=[VM] * 7,
        out_specs=HB,
        out_shape=jax.ShapeDtypeStruct((1024, 1024), bf16),
        scratch_shapes=[pltpu.VMEM((1024, 1024), bf16), pltpu.SemaphoreType.DMA((8,))],
        compiler_params=params(8),
        name="norm",
    )(mine, other, *sqs, gain)


def per_device(inputs, q, k, value_weight, ld, doc_start, gain):
    x, z, core = lax.axis_index("x"), lax.axis_index("z"), lax.axis_index("core")
    first = core == 0
    bar = lax.optimization_barrier

    my_w = lax.dynamic_slice(value_weight, (0, core * HALF), (CHIP // 2, HALF))
    their_w = lax.dynamic_slice(value_weight, (0, (1 - core) * HALF), (CHIP // 2, HALF))
    recv_w = swap(their_w)
    fx, dec, sf = prep(doc_start, ld)
    chip_w = jnp.where(
        first,
        jnp.concatenate([my_w, recv_w, fx], axis=0),
        jnp.concatenate([recv_w, my_w, fx], axis=0),
    )
    chip_w, ld, q, k = bar((chip_w, ld, q, k))
    line = [chip_w] + [crossed(chip_w, "z", "x", d, d) for d in (1, 2, 3)]
    w, kd, xv = pre(ld, q, k, inputs)
    line, w = bar((tuple(line), w))
    p_lo = jnp.concatenate([a[:CHIP] for a in line[:2]] + [a[CHIP:] for a in line], axis=0)
    p_hi = jnp.concatenate([a[:CHIP] for a in line[2:]], axis=0)
    up_lo = crossed(p_lo, "x", "z", 1, 1)
    dn_hi = crossed(p_hi, "x", "z", -1, -1)
    up_hi = crossed(p_hi, "x", "z", 1, 1)
    dn_lo = crossed(p_lo, "x", "z", -1, -1)
    bufs = (p_lo, p_hi, swap(p_lo), swap(p_hi))
    sums, t_own = mm(((True, 0), (False, 0)), xv, bufs, here=True)
    up_lo, dn_hi, sums = bar((up_lo, dn_hi, sums))
    op_lo = crossed(up_lo, "x", "z", 1, 1)
    op_hi = crossed(dn_hi, "x", "z", -1, -1)
    up_lo, up_hi, dn_lo, dn_hi = bar((up_lo, up_hi, dn_lo, dn_hi))
    swapped = (swap(up_lo), swap(up_hi))
    bufs = (up_lo, up_hi, dn_lo, dn_hi)
    mine, t_mine = mm(((True, 1), (True, 3)), xv, bufs, 0, sums, True)
    dn_lo, dn_hi, mine = bar((dn_lo, dn_hi, mine))
    op_lo, op_hi, done = bar((op_lo, op_hi, mine))
    theirs, t_up = mm(((False, 1),), xv, swapped, 1, sums, True)
    theirs, t_dn = mm(((False, 3),), xv, (swap(dn_lo), swap(dn_hi)), -1, theirs, True)
    mine, t_op = mm(((True, 2),), xv, (op_lo, op_hi), -1, done, True)
    bufs = [swap(op_lo), swap(op_hi)]
    v, own, give, t_last, st, qv, wv = post(
        (False, 2), vmem(dec), q, kd, w, mine, theirs, xv, [vmem(a) for a in bufs]
    )
    recv = vmem(swap(give))
    wt = weights(t_own, t_mine, t_op, t_up, t_last, t_dn)
    chip, chip16 = small(chip_kernel, "chip", (wt, own, recv), (f32, bf16))
    got = [vmem(crossed(chip16, "z", "x", d, d)) for d in (1, 2, 3)]
    v, chip = bar((v, chip))
    comb = within(ld, v, st, qv, wv)
    *got, comb = bar((*got, comb))
    sent = small(spread_kernel, "spread", (wt, chip, *got), (f32, bf16, bf16, bf16))
    got = [vmem(crossed(sent[d], "x", "z", d, d)) for d in (1, 2, 3)]
    state, give = small(enter_kernel, "enter", (wt, sent[0], *got, own, recv), (f32, f32))
    sf, qv = vmem(sf), vmem(q)
    mine, sq = outer(0, sf, ld, state, comb, qv)
    other, sq = outer(1, sf, ld, vmem(swap(give)), comb, qv, sq)
    sqs = [sq] + [vmem(ring(sq, "head", d)) for d in (1, 2, 3)]
    return norm(mine, other, sqs, gain.reshape(1, -1))


def solution(mesh):
    mesh = Mesh(mesh.devices.reshape(4, 4, 2, 4), ("x", "z", "core", "head"))
    placed = (
        P(SEQ, None),
        P(SEQ, "head"),
        P(SEQ, "head"),
        P(SEQ, "head"),
        P("head", SEQ),
        P(SEQ),
        P("head"),
    )
    return jax.shard_map(
        per_device, mesh=mesh, in_specs=placed, out_specs=P(SEQ, "head"), check_vma=False
    )
```

```python
import functools
import jax
import jax.numpy as jnp
from jax import lax
from jax.experimental import pallas as pl
from jax.experimental.pallas import tpu as pltpu
from jax.sharding import Mesh, PartitionSpec as P

SHARD_ATTN_PARTS = 32
E = 128
SPAN = 256
SEQ = ("x", "z", "core")
SWAP = [(0, 1), (1, 0)]
VM = pl.BlockSpec(memory_space=pltpu.VMEM)
HB = pl.BlockSpec(memory_space=pltpu.HBM)
MIB = 1024 * 1024
HALF = 512
LINE = 1536
CHIP = 384
ROOM = 2
ROOM_P = 4
f32, bf16 = jnp.float32, jnp.bfloat16


def swap(a):
    return lax.ppermute(a, "core", SWAP)


def ring(a, axis, step):
    return lax.ppermute(a, axis, [(i, (i + step) % 4) for i in range(4)])


def crossed(a, first, second, step0, step1):
    pairs = []
    for x in range(4):
        for z in range(4):
            for c in range(2):
                axis, step = ((first, step0), (second, step1))[c]
                tx = (x + step) % 4 if axis == "x" else x
                tz = (z + step) % 4 if axis == "z" else z
                pairs.append((x * 8 + z * 2 + c, tx * 8 + tz * 2 + c))
    return lax.ppermute(a, SEQ, pairs)


def dot(a, b, dims=((1,), (0,))):
    return lax.dot_general(a, b, (dims, ((), ())), preferred_element_type=f32)


def block_cum(ld):
    lane = lax.broadcasted_iota(jnp.int32, ld.shape, 1)
    step = 1
    while step < SPAN:
        ld = ld + jnp.where(lane >= step, pltpu.roll(ld, step, 1), 0.0)
        step *= 2
    return ld


def vmem(a):
    return pltpu.with_memory_space_constraint(a, pltpu.VMEM)


def hbm(a):
    return pltpu.with_memory_space_constraint(a, pltpu.HBM)


def params(mib):
    return pltpu.CompilerParams(vmem_limit_bytes=mib * MIB)


def prep_kernel(doc_hbm, ld_hbm, fx_ref, dec_ref, sf_ref, doc, ld_ref, sems):
    loads = [
        pltpu.make_async_copy(doc_hbm, doc, sems.at[0]),
        pltpu.make_async_copy(ld_hbm, ld_ref, sems.at[1]),
    ]
    for c in loads:
        c.start()
    for c in loads:
        c.wait()
    lane = lax.broadcasted_iota(jnp.int32, (E, E), 1)
    mat = jnp.zeros((E, E), f32)
    place = lax.broadcasted_iota(jnp.int32, (8, E), 1)
    start = jnp.ones((8, E), f32)
    starts = jnp.zeros((8, E), f32)
    surv = []
    for b in range(4):
        total = jnp.sum(ld_ref[:, b * SPAN : (b + 1) * SPAN], axis=1, keepdims=True)
        decay = jnp.broadcast_to(jnp.exp(total), (8, E))
        dec_ref[b * 8 : b * 8 + 8, :] = decay
        tall = jnp.concatenate([decay, jnp.zeros((E - 8, E), f32)], axis=0)
        mat = jnp.where(lane == b, tall, mat)
        surv.append(1.0 - jnp.full((1, E), doc[b], jnp.int32).astype(f32))
        start = start * surv[b]
        starts = jnp.where(place == b, start, starts)
        start = start * decay
    dec_ref[32:40, :] = jnp.concatenate(surv + [jnp.zeros((4, E), f32)], axis=0)
    rows = jnp.transpose(mat)
    f = None
    for b in range(4):
        f = surv[b] if b == 0 else f * surv[b]
        f = f * rows[b : b + 1, :]
    sf_ref[...] = starts
    high = f.astype(bf16).astype(f32)
    mid = (f - high).astype(bf16).astype(f32)
    low = f - high - mid
    tile = jnp.concatenate([high, mid, low, jnp.zeros((13, E), f32)], axis=0)
    fx_ref[:, E:] = jnp.zeros((16, HALF - E), bf16)
    fx_ref[:, :E] = tile.astype(bf16)


def prep(doc, ld):
    return pl.pallas_call(
        prep_kernel,
        in_specs=[HB, HB],
        out_specs=[VM] * 3,
        out_shape=[
            pltpu.VMEM((16, HALF), bf16),
            jax.ShapeDtypeStruct((40, E), f32),
            jax.ShapeDtypeStruct((8, E), f32),
        ],
        scratch_shapes=[
            pltpu.SMEM(doc.shape, jnp.int32),
            pltpu.VMEM(ld.shape, f32),
            pltpu.SemaphoreType.DMA((2,)),
        ],
        compiler_params=params(4),
        name="prep",
    )(hbm(doc), hbm(ld))


def pre_kernel(
    ld_hbm, q_hbm, k_hbm, x_hbm, w_hbm, kd_hbm, x_ref, q_ref, k_ref, w_ref, kd_ref, ld_ref, *sems
):
    sems, xsems = sems
    decays = pltpu.make_async_copy(ld_hbm, ld_ref, xsems.at[8])
    decays.start()
    half = SPAN // 2
    low = lax.broadcasted_iota(jnp.int32, (half, half), 0) >= lax.broadcasted_iota(
        jnp.int32, (half, half), 1
    )

    def loads(h):
        lanes = pl.ds(pl.multiple_of(h * E, E), E)
        return (
            pltpu.make_async_copy(q_hbm.at[:, lanes], q_ref.at[:, lanes], sems.at[0, h]),
            pltpu.make_async_copy(k_hbm.at[:, lanes], k_ref.at[:, lanes], sems.at[1, h]),
        )

    def stores(h):
        return (
            pltpu.make_async_copy(w_ref.at[h], w_hbm.at[h], sems.at[2, h]),
            pltpu.make_async_copy(kd_ref.at[h], kd_hbm.at[h], sems.at[3, h]),
        )

    for h in range(8):
        for c in loads(h):
            c.start()
    inputs = []
    for r in range(8):
        rows = slice(r * E, (r + 1) * E)
        inputs.append(
            pltpu.make_async_copy(x_hbm.at[rows, :], x_ref.at[rows, :], xsems.at[r])
        )
        inputs[r].start()
    w_ref[:, :, :half, half:] = jnp.zeros((8, 4, half, half), bf16)
    decays.wait()
    cums = [block_cum(ld_ref[:, b * SPAN : (b + 1) * SPAN]) for b in range(4)]

    def one_head(h, carry):
        for c in loads(h):
            c.wait()
        head = lax.broadcasted_iota(jnp.int32, (8, SPAN), 0) == h
        lanes = pl.ds(pl.multiple_of(h * E, E), E)
        for b in range(4):
            row = jnp.sum(jnp.where(head, cums[b], 0.0), axis=0, keepdims=True)
            col = jnp.transpose(jnp.broadcast_to(row, (8, SPAN)))[:, 0:1]
            last = row[:, SPAN - 1 : SPAN]
            rows = slice(b * SPAN, (b + 1) * SPAN)
            k = k_ref[rows, lanes]
            kt = jnp.transpose(k.astype(f32))
            kd_ref[h, b] = (kt * jnp.exp(last - row)).astype(bf16)
            q = q_ref[rows, lanes]
            s = dot(q[:half], k[:half], ((1,), (1,)))
            g = jnp.exp(jnp.where(low, col[:half] - row[:, :half], -1e30))
            w_ref[h, b, :half, :half] = (s * g).astype(bf16)
            s = dot(q[half:], k, ((1,), (1,)))
            g = jnp.exp(col[half:] - row[:, :half])
            w_ref[h, b, half:, :half] = (s[:, :half] * g).astype(bf16)
            g = jnp.exp(jnp.where(low, col[half:] - row[:, half:], -1e30))
            w_ref[h, b, half:, half:] = (s[:, half:] * g).astype(bf16)
        for c in stores(h):
            c.start()
        return carry

    lax.fori_loop(0, 8, one_head, 0)
    for h in range(8):
        for c in stores(h):
            c.wait()
    for c in inputs:
        c.wait()


def pre(ld, q, k, x):
    shapes = ((8, 4, SPAN, SPAN), (8, 4, E, SPAN))
    return pl.pallas_call(
        pre_kernel,
        in_specs=[HB] * 4,
        out_specs=[HB, HB, VM],
        out_shape=[pltpu.HBM(s, bf16) for s in shapes] + [pltpu.VMEM(x.shape, bf16)],
        scratch_shapes=[pltpu.VMEM((1024, 1024), bf16)] * 2
        + [pltpu.VMEM(s, bf16) for s in shapes]
        + [pltpu.VMEM(ld.shape, f32)]
        + [pltpu.SemaphoreType.DMA((4, 8)), pltpu.SemaphoreType.DMA((9,))],
        compiler_params=params(14),
        cost_estimate=pl.CostEstimate(flops=10**9, transcendentals=2 * 10**6, bytes_accessed=10**7),
        name="pre",
    )(hbm(ld), hbm(q), hbm(k), hbm(x))


def multiply(mine, d, x_ref, lo, hi, src, dst):
    x, z, core = lax.axis_index("x"), lax.axis_index("z"), lax.axis_index("core")
    first = (core == 0) if mine else (core == 1)
    line = lax.rem(jnp.where(first, x, z) + 4 - d, 4)
    spans = []
    for e in range(4):
        other = lax.rem(jnp.where(first, z, x) + 4 - e, 4)
        at = jnp.where(first, line * LINE + other * CHIP, other * LINE + line * CHIP)
        spans.append(pl.ds(pl.multiple_of(at, 128), CHIP))
    for r in range(2):
        rows = slice(r * 512, (r + 1) * 512)
        part = src[rows, :] if src is not None else None
        for w, (s0, s1) in ((lo, spans[:2]), (hi, spans[2:])):
            lhs = jnp.concatenate([x_ref[rows, s0], x_ref[rows, s1]], axis=1)
            p = dot(lhs, w[: 2 * CHIP, :])
            part = p if part is None else part + p
        dst[rows, :] = part


def mm_kernel(jobs, plane, here, x_ref, *refs):
    n = 2 * len(jobs)
    bufs, refs = refs[:n], refs[n:]
    src = None
    if plane is not None:
        src = refs[0] if plane < 0 else refs[0].at[plane]
        refs = refs[1:]
    out, tails = refs[:2]
    copies = []
    if here:
        wv = bufs
        for j in range(len(jobs)):
            tails[j] = bufs[2 * j][2 * CHIP :, :E]
    else:
        wv, sems = refs[2:]
        for i, b in enumerate(bufs):
            copies.append(
                pltpu.make_async_copy(b.at[: 2 * CHIP, :], wv.at[i], sems.at[i])
            )
        wv = [wv.at[i] for i in range(n)]
        for j in range(len(jobs)):
            copies.append(
                pltpu.make_async_copy(
                    bufs[2 * j].at[2 * CHIP :, :E], tails.at[j], sems.at[n + j]
                )
            )
    for c in copies:
        c.start()
    for j, (mine, d) in enumerate(jobs):
        for c in copies[2 * j : 2 * j + 2]:
            c.wait()
        if plane is None:
            dst, before = out.at[j], None
        else:
            dst, before = out, (out if j else src)
        multiply(mine, d, x_ref, wv[2 * j], wv[2 * j + 1], before, dst)
    for c in copies[n:]:
        c.wait()


def mm(jobs, x, bufs, plane=None, before=None, here=False):
    n = 2 * len(jobs)
    extra = [] if before is None else [before]
    scratch = [] if here else [
        pltpu.VMEM((n, 2 * CHIP, HALF), bf16),
        pltpu.SemaphoreType.DMA((n + len(jobs),)),
    ]
    return pl.pallas_call(
        functools.partial(mm_kernel, jobs, plane, here),
        in_specs=[VM] + [VM if here else HB] * n + [VM] * len(extra),
        out_specs=[VM] * 2,
        out_shape=[
            pltpu.VMEM((ROOM_P, 1024, HALF) if plane is None else (1024, HALF), f32),
            pltpu.VMEM((len(jobs), 64, E), bf16),
        ],
        scratch_shapes=scratch,
        compiler_params=params(6 if here else 10),
        cost_estimate=pl.CostEstimate(
            flops=1024 * LINE * HALF * n, transcendentals=0, bytes_accessed=n * 5 * 10**6
        ),
        name="project",
    )(x, *[(vmem if here else hbm)(a) for a in bufs], *extra)


def head_col(ld_block):
    return jnp.transpose(jnp.exp(block_cum(ld_block)))


def post_kernel(job, dec, q_hbm, kd_hbm, w_hbm, mine_ref, their_ref, x_ref, lo, hi, *refs):
    v_ref, keep_ref, give_ref, tail_ref, st_ref, q_ref, w_ref, acc, kd_ref, sems = refs
    tail_ref[0] = lo[2 * CHIP :, :E]
    core = lax.axis_index("core")
    loads = [
        pltpu.make_async_copy(s, t, sems.at[i])
        for i, (s, t) in enumerate(((kd_hbm, kd_ref), (q_hbm, q_ref), (w_hbm, w_ref)))
    ]
    for c in loads:
        c.start()
    multiply(*job, x_ref, lo, hi, their_ref, acc)
    loads[0].wait()
    states = [None] * 8
    for b in range(4):
        rows = slice(b * SPAN, (b + 1) * SPAN)
        for h in range(8):
            lanes = slice(h * E, (h + 1) * E)
            part = slice((h % 4) * E, (h % 4 + 1) * E)
            v = jnp.where(core == h // 4, mine_ref[rows, part], acc[rows, part]).astype(bf16)
            v_ref[rows, lanes] = v
            state = states[h]
            if b > 0:
                state = state * dec[32 + b : 33 + b, :]
                high = state.astype(bf16)
                st_ref[h, b - 1, :, :E] = high
                st_ref[h, b - 1, :, E:] = (state - high.astype(f32)).astype(bf16)
            update = dot(kd_ref[h, b], v)
            at = b * 8 + h
            states[h] = update if b == 0 else dec[at : at + 1, :] * state + update
    for h in range(4):
        part = slice(h * E, (h + 1) * E)
        keep_ref[part, :] = jnp.where(core == 0, states[h], states[h + 4])
        give_ref[part, :] = jnp.where(core == 0, states[h + 4], states[h])
    for c in loads[1:]:
        c.wait()


def post(job, dec, q, kd, w, mine, theirs, x, bufs):
    return pl.pallas_call(
        functools.partial(post_kernel, job),
        in_specs=[VM, HB, HB, HB] + [VM] * (3 + len(bufs)),
        out_specs=[VM] * 7,
        out_shape=[
            pltpu.VMEM((1024, 1024), bf16),
            pltpu.VMEM((HALF, E), f32),
            pltpu.VMEM((HALF, E), f32),
            pltpu.VMEM((1, 64, E), bf16),
            pltpu.VMEM((8, 3, E, 2 * E), bf16),
            pltpu.VMEM((1024, 1024), bf16),
            pltpu.VMEM((8, 4, SPAN, SPAN), bf16),
        ],
        scratch_shapes=[
            pltpu.VMEM((1024, HALF), f32),
            pltpu.VMEM((8, 4, E, SPAN), bf16),
            pltpu.SemaphoreType.DMA((3,)),
        ],
        compiler_params=params(10),
        name="post",
    )(dec, hbm(q), hbm(kd), hbm(w), mine, theirs, x, *bufs)


def within_kernel(ld_ref, v_ref, st_ref, q_ref, w_ref, comb_ref):
    half = SPAN // 2
    for b in range(4):
        rows = slice(b * SPAN, (b + 1) * SPAN)
        col = head_col(ld_ref[:, rows])
        for h in range(8):
            lanes = slice(h * E, (h + 1) * E)
            v = v_ref[rows, lanes]
            top = dot(w_ref[h, b, :half, :half], v[:half])
            low = dot(w_ref[h, b, half:, :], v)
            inner = jnp.concatenate([top, low], axis=0)
            if b > 0:
                o = dot(q_ref[rows, lanes], st_ref[h, b - 1])
                inner = inner + col[:, h : h + 1] * (o[:, :E] + o[:, E:])
            comb_ref[0, rows, lanes] = inner


def within(ld, v, st, q, w):
    return pl.pallas_call(
        within_kernel,
        in_specs=[VM] * 5,
        out_specs=VM,
        out_shape=pltpu.VMEM((ROOM, 1024, 1024), f32),
        compiler_params=params(6),
        cost_estimate=pl.CostEstimate(
            flops=3 * 10**9, transcendentals=0, bytes_accessed=10**7
        ),
        name="within",
    )(ld, v, st, q, w)


def weights_kernel(t_own, t_mine, t_op, t_up, t_last, t_dn, out_ref):
    x, z, core = lax.axis_index("x"), lax.axis_index("z"), lax.axis_index("core")
    first = core == 0

    def factors(tiles):
        out = []
        for t in tiles:
            t = t.astype(f32)
            for e in range(4):
                r = [t[16 * e + i : 16 * e + i + 1] for i in range(3)]
                out.append(r[0] + r[1] + r[2])
        return out

    near = factors((t_own[0], t_mine[0], t_op[0], t_mine[1]))
    far = factors((t_own[1], t_up[0], t_last[0], t_dn[0]))
    own = [near[0], far[0]]
    rows = [near[4 * n + e] * far[4 * e + n] for n in range(4) for e in range(4)]
    g = jnp.concatenate(rows, axis=0)
    n = lax.broadcasted_iota(jnp.int32, (16, E), 0)
    px = jnp.where(first, n // 4, n % 4)
    pz = jnp.where(first, n % 4, n // 4)
    k_at = ((x + 4 - px) % 4) * 4 + (z + 4 - pz) % 4
    out = []
    for d in range(4):
        tgt = jnp.where(first, lax.rem(x + d, 4) * 4 + z, x * 4 + lax.rem(z + d, 4))
        for e in range(4):
            src = jnp.where(
                first, x * 4 + lax.rem(z + 4 - e, 4), lax.rem(x + 4 - e, 4) * 4 + z
            )
            p = jnp.where((k_at > src) & (k_at < tgt), g, 1.0)
            p = p[:8] * p[8:]
            p = p[:4] * p[4:]
            p = p[:2] * p[2:]
            p = p[:1] * p[1:]
            out.append(jnp.where(src < tgt, p, 0.0))
    flat = jnp.concatenate(out + own + [jnp.zeros((E - 18, E), f32)], axis=0)
    turned = jnp.transpose(flat)
    out_ref[...] = jnp.where(first, turned[:8], jnp.concatenate([turned[4:8]] * 2, axis=0))


def weights(*tails):
    return pl.pallas_call(
        weights_kernel,
        in_specs=[VM] * 6,
        out_specs=VM,
        out_shape=pltpu.VMEM((8, E), f32),
        compiler_params=params(4),
        name="weights",
    )(*tails)


def one(ref, h, i):
    return jnp.broadcast_to(ref[h : h + 1, i : i + 1], (E, E))


def chip_kernel(wt, own_ref, recv_ref, f_ref, b_ref):
    first = lax.axis_index("core") == 0
    for h in range(4):
        r = slice(h * E, (h + 1) * E)
        a, b = own_ref[r, :], recv_ref[r, :]
        s = jnp.where(first, one(wt, h, 17) * a + b, a + one(wt, h, 16) * b)
        f_ref[r, :] = s
        b_ref[r, :] = s.astype(bf16)


def spread_kernel(wt, own_ref, r1, r2, r3, o0, o1, o2, o3):
    for h in range(4):
        r = slice(h * E, (h + 1) * E)
        src = [own_ref[r, :]] + [a[r, :].astype(f32) for a in (r1, r2, r3)]
        for d, o in enumerate((o0, o1, o2, o3)):
            s = None
            for e in range(4):
                t = one(wt, h, d * 4 + e) * src[e]
                s = t if s is None else s + t
            o[r, :] = s.astype(o.dtype)


def enter_kernel(wt, m0, r1, r2, r3, own_ref, recv_ref, mine_ref, other_ref):
    first = lax.axis_index("core") == 0
    for h in range(4):
        r = slice(h * E, (h + 1) * E)
        i = m0[r, :]
        for a in (r1, r2, r3):
            i = i + a[r, :].astype(f32)
        mine_ref[r, :] = jnp.where(first, i, one(wt, h, 17) * i + recv_ref[r, :])
        other_ref[r, :] = jnp.where(first, one(wt, h, 16) * i + own_ref[r, :], i)


def small(kernel, name, args, outs):
    return pl.pallas_call(
        kernel,
        in_specs=[VM] * len(args),
        out_specs=[VM] * len(outs),
        out_shape=[pltpu.VMEM((HALF, E), t) for t in outs],
        compiler_params=params(4),
        name=name,
    )(*args)


def outer_kernel(side, sf, ld_ref, state_ref, comb_ref, q_ref, *refs):
    before, (out_ref, sq_ref) = refs[:-2], refs[-2:]
    core = lax.axis_index("core")
    half = core if side == 0 else 1 - core
    pairs = []
    for h in range(4):
        m = state_ref[h * E : (h + 1) * E, :]
        high = m.astype(bf16)
        pairs.append(jnp.concatenate([high, (m - high.astype(f32)).astype(bf16)], axis=1))
    for b in range(4):
        rows = slice(b * SPAN, (b + 1) * SPAN)
        scale = jnp.exp(block_cum(ld_ref[:, rows])) * sf[:, b : b + 1]
        scale = jnp.where(half == 0, scale[:4], scale[4:])
        col = jnp.transpose(jnp.concatenate([scale, scale], axis=0))
        total = None
        for h in range(4):
            lanes = pl.ds(pl.multiple_of(half * HALF + h * E, E), E)
            o = dot(q_ref[rows, lanes], pairs[h])
            o = (o[:, :E] + o[:, E:]) * col[:, h : h + 1]
            o = comb_ref[0, rows, lanes] + o
            out_ref[rows, h * E : (h + 1) * E] = o
            total = o * o if total is None else total + o * o
        for t in range(2):
            tt = jnp.transpose(total[t * E : (t + 1) * E, :])
            r = slice(b * 2 + t, b * 2 + t + 1)
            sq = jnp.sum(tt, axis=0, keepdims=True)
            sq_ref[r, :] = sq + before[0][r, :] if before else sq


def outer(side, sf, ld, state, comb, q, *before):
    return pl.pallas_call(
        functools.partial(outer_kernel, side),
        in_specs=[VM] * (5 + len(before)),
        out_specs=[VM, VM],
        out_shape=[pltpu.VMEM((1024, HALF), f32), pltpu.VMEM((8, E), f32)],
        compiler_params=params(6),
        cost_estimate=pl.CostEstimate(
            flops=6 * 10**8, transcendentals=0, bytes_accessed=6 * 10**6
        ),
        name="outer",
    )(sf, ld, state, comb, q, *before)


def norm_kernel(mine_ref, other_ref, s0, s1, s2, s3, gain_ref, y_hbm, y_ref, sems):
    core = lax.axis_index("core")
    total = s0[...] + s1[...] + s2[...] + s3[...]
    scale = lax.rsqrt(total / (SHARD_ATTN_PARTS * E) + 1e-06)
    copies = []
    for t in range(8):
        col = jnp.transpose(jnp.broadcast_to(scale[t : t + 1, :], (E, E)))
        rows = slice(t * E, (t + 1) * E)
        for ref, half in ((mine_ref, core), (other_ref, 1 - core)):
            for h in range(4):
                lanes = pl.ds(pl.multiple_of(half * HALF + h * E, E), E)
                y = ref[rows, h * E : (h + 1) * E] * col * gain_ref[:, lanes]
                y_ref[rows, lanes] = y.astype(bf16)
        c = pltpu.make_async_copy(y_ref.at[rows, :], y_hbm.at[rows, :], sems.at[t])
        c.start()
        copies.append(c)
    for c in copies:
        c.wait()


def norm(mine, other, sqs, gain):
    return pl.pallas_call(
        norm_kernel,
        in_specs=[VM] * 7,
        out_specs=HB,
        out_shape=jax.ShapeDtypeStruct((1024, 1024), bf16),
        scratch_shapes=[pltpu.VMEM((1024, 1024), bf16), pltpu.SemaphoreType.DMA((8,))],
        compiler_params=params(8),
        name="norm",
    )(mine, other, *sqs, gain)


def per_device(inputs, q, k, value_weight, ld, doc_start, gain):
    x, z, core = lax.axis_index("x"), lax.axis_index("z"), lax.axis_index("core")
    first = core == 0
    bar = lax.optimization_barrier

    my_w = lax.dynamic_slice(value_weight, (0, core * HALF), (CHIP // 2, HALF))
    their_w = lax.dynamic_slice(value_weight, (0, (1 - core) * HALF), (CHIP // 2, HALF))
    recv_w = swap(their_w)
    fx, dec, sf = prep(doc_start, ld)
    chip_w = jnp.where(
        first,
        jnp.concatenate([my_w, recv_w, fx], axis=0),
        jnp.concatenate([recv_w, my_w, fx], axis=0),
    )
    chip_w, ld, q, k = bar((chip_w, ld, q, k))
    line = [chip_w] + [crossed(chip_w, "z", "x", d, d) for d in (1, 2, 3)]
    w, kd, xv = pre(ld, q, k, inputs)
    line, w = bar((tuple(line), w))
    p_lo = jnp.concatenate([a[:CHIP] for a in line[:2]] + [a[CHIP:] for a in line], axis=0)
    p_hi = jnp.concatenate([a[:CHIP] for a in line[2:]], axis=0)
    up_lo = crossed(p_lo, "x", "z", 1, 1)
    dn_hi = crossed(p_hi, "x", "z", -1, -1)
    up_hi = crossed(p_hi, "x", "z", 1, 1)
    dn_lo = crossed(p_lo, "x", "z", -1, -1)
    bufs = (p_lo, p_hi, swap(p_lo), swap(p_hi))
    sums, t_own = mm(((True, 0), (False, 0)), xv, bufs, here=True)
    up_lo, dn_hi, sums = bar((up_lo, dn_hi, sums))
    op_lo = crossed(up_lo, "x", "z", 1, 1)
    op_hi = crossed(dn_hi, "x", "z", -1, -1)
    up_lo, up_hi, dn_lo, dn_hi = bar((up_lo, up_hi, dn_lo, dn_hi))
    swapped = (swap(up_lo), swap(up_hi))
    bufs = (up_lo, up_hi, dn_lo, dn_hi)
    mine, t_mine = mm(((True, 1), (True, 3)), xv, bufs, 0, sums, True)
    dn_lo, dn_hi, mine = bar((dn_lo, dn_hi, mine))
    op_lo, op_hi, done = bar((op_lo, op_hi, mine))
    theirs, t_up = mm(((False, 1),), xv, swapped, 1, sums, True)
    theirs, t_dn = mm(((False, 3),), xv, (swap(dn_lo), swap(dn_hi)), -1, theirs, True)
    mine, t_op = mm(((True, 2),), xv, (op_lo, op_hi), -1, done, True)
    bufs = [swap(op_lo), swap(op_hi)]
    v, own, give, t_last, st, qv, wv = post(
        (False, 2), vmem(dec), q, kd, w, mine, theirs, xv, [vmem(a) for a in bufs]
    )
    recv = vmem(swap(give))
    wt = weights(t_own, t_mine, t_op, t_up, t_last, t_dn)
    chip, chip16 = small(chip_kernel, "chip", (wt, own, recv), (f32, bf16))
    got = [vmem(crossed(chip16, "z", "x", d, d)) for d in (1, 2, 3)]
    v, chip = bar((v, chip))
    comb = within(ld, v, st, qv, wv)
    *got, comb = bar((*got, comb))
    sent = small(spread_kernel, "spread", (wt, chip, *got), (f32, bf16, bf16, bf16))
    got = [vmem(crossed(sent[d], "x", "z", d, d)) for d in (1, 2, 3)]
    state, give = small(enter_kernel, "enter", (wt, sent[0], *got, own, recv), (f32, f32))
    sf, qv = vmem(sf), vmem(q)
    mine, sq = outer(0, sf, ld, state, comb, qv)
    other, sq = outer(1, sf, ld, vmem(swap(give)), comb, qv, sq)
    sqs = [sq] + [vmem(ring(sq, "head", d)) for d in (1, 2, 3)]
    return norm(mine, other, sqs, gain.reshape(1, -1))


def solution(mesh):
    mesh = Mesh(mesh.devices.reshape(4, 4, 2, 4), ("x", "z", "core", "head"))
    placed = (
        P(SEQ, None),
        P(SEQ, "head"),
        P(SEQ, "head"),
        P(SEQ, "head"),
        P("head", SEQ),
        P(SEQ),
        P("head"),
    )
    return jax.shard_map(
        per_device, mesh=mesh, in_specs=placed, out_specs=P(SEQ, "head"), check_vma=False
    )
```

```python
import functools
import jax
import jax.numpy as jnp
from jax import lax
from jax.experimental import pallas as pl
from jax.experimental.pallas import tpu as pltpu
from jax.sharding import Mesh, PartitionSpec as P

SHARD_ATTN_PARTS = 32
E = 128
SPAN = 256
SEQ = ("x", "z", "core")
SWAP = [(0, 1), (1, 0)]
VM = pl.BlockSpec(memory_space=pltpu.VMEM)
HB = pl.BlockSpec(memory_space=pltpu.HBM)
MIB = 1024 * 1024
HALF = 512
LINE = 1536
CHIP = 384
ROOM = 2
ROOM_P = 4
f32, bf16 = jnp.float32, jnp.bfloat16


def swap(a):
    return lax.ppermute(a, "core", SWAP)


def ring(a, axis, step):
    return lax.ppermute(a, axis, [(i, (i + step) % 4) for i in range(4)])


def crossed(a, first, second, step0, step1):
    pairs = []
    for x in range(4):
        for z in range(4):
            for c in range(2):
                axis, step = ((first, step0), (second, step1))[c]
                tx = (x + step) % 4 if axis == "x" else x
                tz = (z + step) % 4 if axis == "z" else z
                pairs.append((x * 8 + z * 2 + c, tx * 8 + tz * 2 + c))
    return lax.ppermute(a, SEQ, pairs)


def dot(a, b, dims=((1,), (0,))):
    return lax.dot_general(a, b, (dims, ((), ())), preferred_element_type=f32)


def block_cum(ld):
    lane = lax.broadcasted_iota(jnp.int32, ld.shape, 1)
    step = 1
    while step < SPAN:
        ld = ld + jnp.where(lane >= step, pltpu.roll(ld, step, 1), 0.0)
        step *= 2
    return ld


def vmem(a):
    return pltpu.with_memory_space_constraint(a, pltpu.VMEM)


def hbm(a):
    return pltpu.with_memory_space_constraint(a, pltpu.HBM)


def params(mib):
    return pltpu.CompilerParams(vmem_limit_bytes=mib * MIB)


def prep_kernel(doc_hbm, ld_hbm, fx_ref, dec_ref, sf_ref, doc, ld_ref, sems):
    loads = [
        pltpu.make_async_copy(doc_hbm, doc, sems.at[0]),
        pltpu.make_async_copy(ld_hbm, ld_ref, sems.at[1]),
    ]
    for c in loads:
        c.start()
    for c in loads:
        c.wait()
    lane = lax.broadcasted_iota(jnp.int32, (E, E), 1)
    mat = jnp.zeros((E, E), f32)
    place = lax.broadcasted_iota(jnp.int32, (8, E), 1)
    start = jnp.ones((8, E), f32)
    starts = jnp.zeros((8, E), f32)
    surv = []
    for b in range(4):
        total = jnp.sum(ld_ref[:, b * SPAN : (b + 1) * SPAN], axis=1, keepdims=True)
        decay = jnp.broadcast_to(jnp.exp(total), (8, E))
        dec_ref[b * 8 : b * 8 + 8, :] = decay
        tall = jnp.concatenate([decay, jnp.zeros((E - 8, E), f32)], axis=0)
        mat = jnp.where(lane == b, tall, mat)
        surv.append(1.0 - jnp.full((1, E), doc[b], jnp.int32).astype(f32))
        start = start * surv[b]
        starts = jnp.where(place == b, start, starts)
        start = start * decay
    dec_ref[32:40, :] = jnp.concatenate(surv + [jnp.zeros((4, E), f32)], axis=0)
    rows = jnp.transpose(mat)
    f = None
    for b in range(4):
        f = surv[b] if b == 0 else f * surv[b]
        f = f * rows[b : b + 1, :]
    sf_ref[...] = starts
    high = f.astype(bf16).astype(f32)
    mid = (f - high).astype(bf16).astype(f32)
    low = f - high - mid
    tile = jnp.concatenate([high, mid, low, jnp.zeros((13, E), f32)], axis=0)
    fx_ref[:, E:] = jnp.zeros((16, HALF - E), bf16)
    fx_ref[:, :E] = tile.astype(bf16)


def prep(doc, ld):
    return pl.pallas_call(
        prep_kernel,
        in_specs=[HB, HB],
        out_specs=[VM] * 3,
        out_shape=[
            pltpu.VMEM((16, HALF), bf16),
            jax.ShapeDtypeStruct((40, E), f32),
            jax.ShapeDtypeStruct((8, E), f32),
        ],
        scratch_shapes=[
            pltpu.SMEM(doc.shape, jnp.int32),
            pltpu.VMEM(ld.shape, f32),
            pltpu.SemaphoreType.DMA((2,)),
        ],
        compiler_params=params(4),
        name="prep",
    )(hbm(doc), hbm(ld))


def pre_kernel(
    ld_hbm, q_hbm, k_hbm, x_hbm, w_hbm, kd_hbm, x_ref, q_ref, k_ref, w_ref, kd_ref, ld_ref, *sems
):
    sems, xsems = sems
    decays = pltpu.make_async_copy(ld_hbm, ld_ref, xsems.at[8])
    decays.start()
    half = SPAN // 2
    low = lax.broadcasted_iota(jnp.int32, (half, half), 0) >= lax.broadcasted_iota(
        jnp.int32, (half, half), 1
    )

    def loads(h):
        lanes = pl.ds(pl.multiple_of(h * E, E), E)
        return (
            pltpu.make_async_copy(q_hbm.at[:, lanes], q_ref.at[:, lanes], sems.at[0, h]),
            pltpu.make_async_copy(k_hbm.at[:, lanes], k_ref.at[:, lanes], sems.at[1, h]),
        )

    def stores(h):
        return (
            pltpu.make_async_copy(w_ref.at[h], w_hbm.at[h], sems.at[2, h]),
            pltpu.make_async_copy(kd_ref.at[h], kd_hbm.at[h], sems.at[3, h]),
        )

    for h in range(8):
        for c in loads(h):
            c.start()
    inputs = []
    for r in range(8):
        rows = slice(r * E, (r + 1) * E)
        inputs.append(
            pltpu.make_async_copy(x_hbm.at[rows, :], x_ref.at[rows, :], xsems.at[r])
        )
        inputs[r].start()
    w_ref[:, :, :half, half:] = jnp.zeros((8, 4, half, half), bf16)
    decays.wait()
    cums = [block_cum(ld_ref[:, b * SPAN : (b + 1) * SPAN]) for b in range(4)]

    def one_head(h, carry):
        for c in loads(h):
            c.wait()
        head = lax.broadcasted_iota(jnp.int32, (8, SPAN), 0) == h
        lanes = pl.ds(pl.multiple_of(h * E, E), E)
        for b in range(4):
            row = jnp.sum(jnp.where(head, cums[b], 0.0), axis=0, keepdims=True)
            col = jnp.transpose(jnp.broadcast_to(row, (8, SPAN)))[:, 0:1]
            last = row[:, SPAN - 1 : SPAN]
            rows = slice(b * SPAN, (b + 1) * SPAN)
            k = k_ref[rows, lanes]
            kt = jnp.transpose(k.astype(f32))
            kd_ref[h, b] = (kt * jnp.exp(last - row)).astype(bf16)
            q = q_ref[rows, lanes]
            s = dot(q[:half], k[:half], ((1,), (1,)))
            g = jnp.exp(jnp.where(low, col[:half] - row[:, :half], -1e30))
            w_ref[h, b, :half, :half] = (s * g).astype(bf16)
            s = dot(q[half:], k, ((1,), (1,)))
            g = jnp.exp(col[half:] - row[:, :half])
            w_ref[h, b, half:, :half] = (s[:, :half] * g).astype(bf16)
            g = jnp.exp(jnp.where(low, col[half:] - row[:, half:], -1e30))
            w_ref[h, b, half:, half:] = (s[:, half:] * g).astype(bf16)
        for c in stores(h):
            c.start()
        return carry

    lax.fori_loop(0, 8, one_head, 0)
    for h in range(8):
        for c in stores(h):
            c.wait()
    for c in inputs:
        c.wait()


def pre(ld, q, k, x):
    shapes = ((8, 4, SPAN, SPAN), (8, 4, E, SPAN))
    return pl.pallas_call(
        pre_kernel,
        in_specs=[HB] * 4,
        out_specs=[HB, HB, VM],
        out_shape=[pltpu.HBM(s, bf16) for s in shapes] + [pltpu.VMEM(x.shape, bf16)],
        scratch_shapes=[pltpu.VMEM((1024, 1024), bf16)] * 2
        + [pltpu.VMEM(s, bf16) for s in shapes]
        + [pltpu.VMEM(ld.shape, f32)]
        + [pltpu.SemaphoreType.DMA((4, 8)), pltpu.SemaphoreType.DMA((9,))],
        compiler_params=params(14),
        cost_estimate=pl.CostEstimate(flops=10**9, transcendentals=2 * 10**6, bytes_accessed=10**7),
        name="pre",
    )(hbm(ld), hbm(q), hbm(k), hbm(x))


def multiply(mine, d, x_ref, lo, hi, src, dst):
    x, z, core = lax.axis_index("x"), lax.axis_index("z"), lax.axis_index("core")
    first = (core == 0) if mine else (core == 1)
    line = lax.rem(jnp.where(first, x, z) + 4 - d, 4)
    spans = []
    for e in range(4):
        other = lax.rem(jnp.where(first, z, x) + 4 - e, 4)
        at = jnp.where(first, line * LINE + other * CHIP, other * LINE + line * CHIP)
        spans.append(pl.ds(pl.multiple_of(at, 128), CHIP))
    for r in range(2):
        rows = slice(r * 512, (r + 1) * 512)
        part = src[rows, :] if src is not None else None
        for w, (s0, s1) in ((lo, spans[:2]), (hi, spans[2:])):
            lhs = jnp.concatenate([x_ref[rows, s0], x_ref[rows, s1]], axis=1)
            p = dot(lhs, w[: 2 * CHIP, :])
            part = p if part is None else part + p
        dst[rows, :] = part


def mm_kernel(jobs, plane, here, x_ref, *refs):
    n = 2 * len(jobs)
    bufs, refs = refs[:n], refs[n:]
    src = None
    if plane is not None:
        src = refs[0] if plane < 0 else refs[0].at[plane]
        refs = refs[1:]
    out, tails = refs[:2]
    copies = []
    if here:
        wv = bufs
        for j in range(len(jobs)):
            tails[j] = bufs[2 * j][2 * CHIP :, :E]
    else:
        wv, sems = refs[2:]
        for i, b in enumerate(bufs):
            copies.append(
                pltpu.make_async_copy(b.at[: 2 * CHIP, :], wv.at[i], sems.at[i])
            )
        wv = [wv.at[i] for i in range(n)]
        for j in range(len(jobs)):
            copies.append(
                pltpu.make_async_copy(
                    bufs[2 * j].at[2 * CHIP :, :E], tails.at[j], sems.at[n + j]
                )
            )
    for c in copies:
        c.start()
    for j, (mine, d) in enumerate(jobs):
        for c in copies[2 * j : 2 * j + 2]:
            c.wait()
        if plane is None:
            dst, before = out.at[j], None
        else:
            dst, before = out, (out if j else src)
        multiply(mine, d, x_ref, wv[2 * j], wv[2 * j + 1], before, dst)
    for c in copies[n:]:
        c.wait()


def mm(jobs, x, bufs, plane=None, before=None, here=False):
    n = 2 * len(jobs)
    extra = [] if before is None else [before]
    scratch = [] if here else [
        pltpu.VMEM((n, 2 * CHIP, HALF), bf16),
        pltpu.SemaphoreType.DMA((n + len(jobs),)),
    ]
    return pl.pallas_call(
        functools.partial(mm_kernel, jobs, plane, here),
        in_specs=[VM] + [VM if here else HB] * n + [VM] * len(extra),
        out_specs=[VM] * 2,
        out_shape=[
            pltpu.VMEM((ROOM_P, 1024, HALF) if plane is None else (1024, HALF), f32),
            pltpu.VMEM((len(jobs), 64, E), bf16),
        ],
        scratch_shapes=scratch,
        compiler_params=params(6 if here else 10),
        cost_estimate=pl.CostEstimate(
            flops=1024 * LINE * HALF * n, transcendentals=0, bytes_accessed=n * 5 * 10**6
        ),
        name="project",
    )(x, *[(vmem if here else hbm)(a) for a in bufs], *extra)


def head_col(ld_block):
    return jnp.transpose(jnp.exp(block_cum(ld_block)))


def post_kernel(job, dec, q_hbm, kd_hbm, w_hbm, mine_ref, their_ref, x_ref, lo, hi, *refs):
    v_ref, keep_ref, give_ref, tail_ref, st_ref, q_ref, w_ref, acc, kd_ref, sems = refs
    tail_ref[0] = lo[2 * CHIP :, :E]
    core = lax.axis_index("core")
    loads = [
        pltpu.make_async_copy(s, t, sems.at[i])
        for i, (s, t) in enumerate(((kd_hbm, kd_ref), (q_hbm, q_ref), (w_hbm, w_ref)))
    ]
    for c in loads:
        c.start()
    multiply(*job, x_ref, lo, hi, their_ref, acc)
    loads[0].wait()
    states = [None] * 8
    for b in range(4):
        rows = slice(b * SPAN, (b + 1) * SPAN)
        for h in range(8):
            lanes = slice(h * E, (h + 1) * E)
            part = slice((h % 4) * E, (h % 4 + 1) * E)
            v = jnp.where(core == h // 4, mine_ref[rows, part], acc[rows, part]).astype(bf16)
            v_ref[rows, lanes] = v
            state = states[h]
            if b > 0:
                state = state * dec[32 + b : 33 + b, :]
                high = state.astype(bf16)
                st_ref[h, b - 1, :, :E] = high
                st_ref[h, b - 1, :, E:] = (state - high.astype(f32)).astype(bf16)
            update = dot(kd_ref[h, b], v)
            at = b * 8 + h
            states[h] = update if b == 0 else dec[at : at + 1, :] * state + update
    for h in range(4):
        part = slice(h * E, (h + 1) * E)
        keep_ref[part, :] = jnp.where(core == 0, states[h], states[h + 4])
        give_ref[part, :] = jnp.where(core == 0, states[h + 4], states[h])
    for c in loads[1:]:
        c.wait()


def post(job, dec, q, kd, w, mine, theirs, x, bufs):
    return pl.pallas_call(
        functools.partial(post_kernel, job),
        in_specs=[VM, HB, HB, HB] + [VM] * (3 + len(bufs)),
        out_specs=[VM] * 7,
        out_shape=[
            pltpu.VMEM((1024, 1024), bf16),
            pltpu.VMEM((HALF, E), f32),
            pltpu.VMEM((HALF, E), f32),
            pltpu.VMEM((1, 64, E), bf16),
            pltpu.VMEM((8, 3, E, 2 * E), bf16),
            pltpu.VMEM((1024, 1024), bf16),
            pltpu.VMEM((8, 4, SPAN, SPAN), bf16),
        ],
        scratch_shapes=[
            pltpu.VMEM((1024, HALF), f32),
            pltpu.VMEM((8, 4, E, SPAN), bf16),
            pltpu.SemaphoreType.DMA((3,)),
        ],
        compiler_params=params(10),
        name="post",
    )(dec, hbm(q), hbm(kd), hbm(w), mine, theirs, x, *bufs)


def within_kernel(ld_ref, v_ref, st_ref, q_ref, w_ref, comb_ref):
    half = SPAN // 2
    for b in range(4):
        rows = slice(b * SPAN, (b + 1) * SPAN)
        col = head_col(ld_ref[:, rows])
        for h in range(8):
            lanes = slice(h * E, (h + 1) * E)
            v = v_ref[rows, lanes]
            top = dot(w_ref[h, b, :half, :half], v[:half])
            low = dot(w_ref[h, b, half:, :], v)
            inner = jnp.concatenate([top, low], axis=0)
            if b > 0:
                o = dot(q_ref[rows, lanes], st_ref[h, b - 1])
                inner = inner + col[:, h : h + 1] * (o[:, :E] + o[:, E:])
            comb_ref[0, rows, lanes] = inner


def within(ld, v, st, q, w):
    return pl.pallas_call(
        within_kernel,
        in_specs=[VM] * 5,
        out_specs=VM,
        out_shape=pltpu.VMEM((ROOM, 1024, 1024), f32),
        compiler_params=params(6),
        cost_estimate=pl.CostEstimate(
            flops=3 * 10**9, transcendentals=0, bytes_accessed=10**7
        ),
        name="within",
    )(ld, v, st, q, w)


def weights_kernel(t_own, t_mine, t_op, t_up, t_last, t_dn, out_ref):
    x, z, core = lax.axis_index("x"), lax.axis_index("z"), lax.axis_index("core")
    first = core == 0

    def factors(tiles):
        out = []
        for t in tiles:
            t = t.astype(f32)
            for e in range(4):
                r = [t[16 * e + i : 16 * e + i + 1] for i in range(3)]
                out.append(r[0] + r[1] + r[2])
        return out

    near = factors((t_own[0], t_mine[0], t_op[0], t_mine[1]))
    far = factors((t_own[1], t_up[0], t_last[0], t_dn[0]))
    own = [near[0], far[0]]
    rows = [near[4 * n + e] * far[4 * e + n] for n in range(4) for e in range(4)]
    g = jnp.concatenate(rows, axis=0)
    n = lax.broadcasted_iota(jnp.int32, (16, E), 0)
    px = jnp.where(first, n // 4, n % 4)
    pz = jnp.where(first, n % 4, n // 4)
    k_at = ((x + 4 - px) % 4) * 4 + (z + 4 - pz) % 4
    out = []
    for d in range(4):
        tgt = jnp.where(first, lax.rem(x + d, 4) * 4 + z, x * 4 + lax.rem(z + d, 4))
        for e in range(4):
            src = jnp.where(
                first, x * 4 + lax.rem(z + 4 - e, 4), lax.rem(x + 4 - e, 4) * 4 + z
            )
            p = jnp.where((k_at > src) & (k_at < tgt), g, 1.0)
            p = p[:8] * p[8:]
            p = p[:4] * p[4:]
            p = p[:2] * p[2:]
            p = p[:1] * p[1:]
            out.append(jnp.where(src < tgt, p, 0.0))
    flat = jnp.concatenate(out + own + [jnp.zeros((E - 18, E), f32)], axis=0)
    turned = jnp.transpose(flat)
    out_ref[...] = jnp.where(first, turned[:8], jnp.concatenate([turned[4:8]] * 2, axis=0))


def weights(*tails):
    return pl.pallas_call(
        weights_kernel,
        in_specs=[VM] * 6,
        out_specs=VM,
        out_shape=pltpu.VMEM((8, E), f32),
        compiler_params=params(4),
        name="weights",
    )(*tails)


def one(ref, h, i):
    return jnp.broadcast_to(ref[h : h + 1, i : i + 1], (E, E))


def chip_kernel(wt, own_ref, recv_ref, f_ref, b_ref):
    first = lax.axis_index("core") == 0
    for h in range(4):
        r = slice(h * E, (h + 1) * E)
        a, b = own_ref[r, :], recv_ref[r, :]
        s = jnp.where(first, one(wt, h, 17) * a + b, a + one(wt, h, 16) * b)
        f_ref[r, :] = s
        b_ref[r, :] = s.astype(bf16)


def spread_kernel(wt, own_ref, r1, r2, r3, o0, o1, o2, o3):
    for h in range(4):
        r = slice(h * E, (h + 1) * E)
        src = [own_ref[r, :]] + [a[r, :].astype(f32) for a in (r1, r2, r3)]
        for d, o in enumerate((o0, o1, o2, o3)):
            s = None
            for e in range(4):
                t = one(wt, h, d * 4 + e) * src[e]
                s = t if s is None else s + t
            o[r, :] = s.astype(o.dtype)


def enter_kernel(wt, m0, r1, r2, r3, own_ref, recv_ref, mine_ref, other_ref):
    first = lax.axis_index("core") == 0
    for h in range(4):
        r = slice(h * E, (h + 1) * E)
        i = m0[r, :]
        for a in (r1, r2, r3):
            i = i + a[r, :].astype(f32)
        mine_ref[r, :] = jnp.where(first, i, one(wt, h, 17) * i + recv_ref[r, :])
        other_ref[r, :] = jnp.where(first, one(wt, h, 16) * i + own_ref[r, :], i)


def small(kernel, name, args, outs):
    return pl.pallas_call(
        kernel,
        in_specs=[VM] * len(args),
        out_specs=[VM] * len(outs),
        out_shape=[pltpu.VMEM((HALF, E), t) for t in outs],
        compiler_params=params(4),
        name=name,
    )(*args)


def outer_kernel(side, sf, ld_ref, state_ref, comb_ref, q_ref, *refs):
    before, (out_ref, sq_ref) = refs[:-2], refs[-2:]
    core = lax.axis_index("core")
    half = core if side == 0 else 1 - core
    pairs = []
    for h in range(4):
        m = state_ref[h * E : (h + 1) * E, :]
        high = m.astype(bf16)
        pairs.append(jnp.concatenate([high, (m - high.astype(f32)).astype(bf16)], axis=1))
    for b in range(4):
        rows = slice(b * SPAN, (b + 1) * SPAN)
        scale = jnp.exp(block_cum(ld_ref[:, rows])) * sf[:, b : b + 1]
        scale = jnp.where(half == 0, scale[:4], scale[4:])
        col = jnp.transpose(jnp.concatenate([scale, scale], axis=0))
        total = None
        for h in range(4):
            lanes = pl.ds(pl.multiple_of(half * HALF + h * E, E), E)
            o = dot(q_ref[rows, lanes], pairs[h])
            o = (o[:, :E] + o[:, E:]) * col[:, h : h + 1]
            o = comb_ref[0, rows, lanes] + o
            out_ref[rows, h * E : (h + 1) * E] = o
            total = o * o if total is None else total + o * o
        for t in range(2):
            tt = jnp.transpose(total[t * E : (t + 1) * E, :])
            r = slice(b * 2 + t, b * 2 + t + 1)
            sq = jnp.sum(tt, axis=0, keepdims=True)
            sq_ref[r, :] = sq + before[0][r, :] if before else sq


def outer(side, sf, ld, state, comb, q, *before):
    return pl.pallas_call(
        functools.partial(outer_kernel, side),
        in_specs=[VM] * (5 + len(before)),
        out_specs=[VM, VM],
        out_shape=[pltpu.VMEM((1024, HALF), f32), pltpu.VMEM((8, E), f32)],
        compiler_params=params(6),
        cost_estimate=pl.CostEstimate(
            flops=6 * 10**8, transcendentals=0, bytes_accessed=6 * 10**6
        ),
        name="outer",
    )(sf, ld, state, comb, q, *before)


def norm_kernel(mine_ref, other_ref, s0, s1, s2, s3, gain_ref, y_hbm, y_ref, sems):
    core = lax.axis_index("core")
    total = s0[...] + s1[...] + s2[...] + s3[...]
    scale = lax.rsqrt(total / (SHARD_ATTN_PARTS * E) + 1e-06)
    copies = []
    for t in range(8):
        col = jnp.transpose(jnp.broadcast_to(scale[t : t + 1, :], (E, E)))
        rows = slice(t * E, (t + 1) * E)
        for ref, half in ((mine_ref, core), (other_ref, 1 - core)):
            for h in range(4):
                lanes = pl.ds(pl.multiple_of(half * HALF + h * E, E), E)
                y = ref[rows, h * E : (h + 1) * E] * col * gain_ref[:, lanes]
                y_ref[rows, lanes] = y.astype(bf16)
        c = pltpu.make_async_copy(y_ref.at[rows, :], y_hbm.at[rows, :], sems.at[t])
        c.start()
        copies.append(c)
    for c in copies:
        c.wait()


def norm(mine, other, sqs, gain):
    return pl.pallas_call(
        norm_kernel,
        in_specs=[VM] * 7,
        out_specs=HB,
        out_shape=jax.ShapeDtypeStruct((1024, 1024), bf16),
        scratch_shapes=[pltpu.VMEM((1024, 1024), bf16), pltpu.SemaphoreType.DMA((8,))],
        compiler_params=params(8),
        name="norm",
    )(mine, other, *sqs, gain)


def per_device(inputs, q, k, value_weight, ld, doc_start, gain):
    x, z, core = lax.axis_index("x"), lax.axis_index("z"), lax.axis_index("core")
    first = core == 0
    bar = lax.optimization_barrier

    my_w = lax.dynamic_slice(value_weight, (0, core * HALF), (CHIP // 2, HALF))
    their_w = lax.dynamic_slice(value_weight, (0, (1 - core) * HALF), (CHIP // 2, HALF))
    recv_w = swap(their_w)
    fx, dec, sf = prep(doc_start, ld)
    chip_w = jnp.where(
        first,
        jnp.concatenate([my_w, recv_w, fx], axis=0),
        jnp.concatenate([recv_w, my_w, fx], axis=0),
    )
    chip_w, ld, q, k = bar((chip_w, ld, q, k))
    line = [chip_w] + [crossed(chip_w, "z", "x", d, d) for d in (1, 2, 3)]
    w, kd, xv = pre(ld, q, k, inputs)
    line, w = bar((tuple(line), w))
    p_lo = jnp.concatenate([a[:CHIP] for a in line[:2]] + [a[CHIP:] for a in line], axis=0)
    p_hi = jnp.concatenate([a[:CHIP] for a in line[2:]], axis=0)
    up_lo = crossed(p_lo, "x", "z", 1, 1)
    dn_hi = crossed(p_hi, "x", "z", -1, -1)
    up_hi = crossed(p_hi, "x", "z", 1, 1)
    dn_lo = crossed(p_lo, "x", "z", -1, -1)
    bufs = (p_lo, p_hi, swap(p_lo), swap(p_hi))
    sums, t_own = mm(((True, 0), (False, 0)), xv, bufs, here=True)
    up_lo, dn_hi, sums = bar((up_lo, dn_hi, sums))
    op_lo = crossed(up_lo, "x", "z", 1, 1)
    op_hi = crossed(dn_hi, "x", "z", -1, -1)
    up_lo, up_hi, dn_lo, dn_hi = bar((up_lo, up_hi, dn_lo, dn_hi))
    swapped = (swap(up_lo), swap(up_hi))
    bufs = (up_lo, up_hi, dn_lo, dn_hi)
    mine, t_mine = mm(((True, 1), (True, 3)), xv, bufs, 0, sums, True)
    dn_lo, dn_hi, mine = bar((dn_lo, dn_hi, mine))
    op_lo, op_hi, done = bar((op_lo, op_hi, mine))
    theirs, t_up = mm(((False, 1),), xv, swapped, 1, sums, True)
    theirs, t_dn = mm(((False, 3),), xv, (swap(dn_lo), swap(dn_hi)), -1, theirs, True)
    mine, t_op = mm(((True, 2),), xv, (op_lo, op_hi), -1, done, True)
    bufs = [swap(op_lo), swap(op_hi)]
    v, own, give, t_last, st, qv, wv = post(
        (False, 2), vmem(dec), q, kd, w, mine, theirs, xv, [vmem(a) for a in bufs]
    )
    recv = vmem(swap(give))
    wt = weights(t_own, t_mine, t_op, t_up, t_last, t_dn)
    chip, chip16 = small(chip_kernel, "chip", (wt, own, recv), (f32, bf16))
    got = [vmem(crossed(chip16, "z", "x", d, d)) for d in (1, 2, 3)]
    v, chip = bar((v, chip))
    comb = within(ld, v, st, qv, wv)
    *got, comb = bar((*got, comb))
    sent = small(spread_kernel, "spread", (wt, chip, *got), (f32, bf16, bf16, bf16))
    got = [vmem(crossed(sent[d], "x", "z", d, d)) for d in (1, 2, 3)]
    state, give = small(enter_kernel, "enter", (wt, sent[0], *got, own, recv), (f32, f32))
    sf, qv = vmem(sf), vmem(q)
    mine, sq = outer(0, sf, ld, state, comb, qv)
    other, sq = outer(1, sf, ld, vmem(swap(give)), comb, qv, sq)
    sqs = [sq] + [vmem(ring(sq, "head", d)) for d in (2, 1, 3)]
    return norm(mine, other, sqs, gain.reshape(1, -1))


def solution(mesh):
    mesh = Mesh(mesh.devices.reshape(4, 4, 2, 4), ("x", "z", "core", "head"))
    placed = (
        P(SEQ, None),
        P(SEQ, "head"),
        P(SEQ, "head"),
        P(SEQ, "head"),
        P("head", SEQ),
        P(SEQ),
        P("head"),
    )
    return jax.shard_map(
        per_device, mesh=mesh, in_specs=placed, out_specs=P(SEQ, "head"), check_vma=False
    )
```
